512 devices in a mesh: dp: 32 (over z, x), fsdp: 16 (over y, core).
Axes of the slice: x: 4, y: 8, z: 8, core: 2. Of those that a mesh axis runs over, the one named last changes fastest.
Arguments:
- hidden_states: bfloat16 [8192, 8192], P('dp'), may hold values from -8 to 8
- lengths: int32 [64], P('dp'), may hold values from 32 to 128, as said below
- labels: int32 [64], P('dp'), may hold values from 0 to 1, as said below
- token_mask: int32 [8192], P('dp'), may hold values from 0 to 1, as said below
- q_weight: bfloat16 [8192, 4096], P('dp', 'fsdp'), may hold values from -0.0625 to 0.0625
- k_weight: bfloat16 [8192, 512], P('dp', 'fsdp'), may hold values from -0.0625 to 0.0625
- v_weight: bfloat16 [8192, 512], P('dp', 'fsdp'), may hold values from -0.0625 to 0.0625
- q_down: bfloat16 [8192, 64], P('dp'), may hold values from -0.0625 to 0.0625
- v_down: bfloat16 [8192, 64], P('dp'), may hold values from -0.0625 to 0.0625
- query_up_weight: bfloat16 [64, 4096], P(None, 'fsdp'), may hold values from -0.29882812 to 0.29882812
- value_up_weight: bfloat16 [64, 512], P(None, 'fsdp'), may hold values from -0.29882812 to 0.29882812
- out_grad: bfloat16 [8192, 4096], P('dp', 'fsdp'), may hold values from -0.52734375 to 0.52734375
Outputs:
- q_down_grad: float32 [8192, 64], P('dp')
- v_down_grad: float32 [8192, 64], P('dp')
- query_up_gradient: float32 [64, 4096], P('dp', 'fsdp')
- value_up_gradient: float32 [64, 512], P('dp', 'fsdp')
The draws below stay inside these ranges and needn't reach their ends.
Inputs may be any that keep to these rules, and one draw needn't show every extreme that they name: `lengths`: some prompt has exactly 128 live positions. `labels`: exactly half of the prompts are harmful. `token_mask`: zero at positions at or past the prompt's length, one at its last live position.
All inputs are finite; a program needn't handle non-finite values.
Results may differ from the reference program's by a relative error of at most 0.018.
The reference program's roundings to bfloat16 on the way count: a program that leaves them out, or rounds other values in their place, can miss the bound.
Values may be sent and summed in bfloat16 or wider, within the bound.
A program may use at most 64 MiB of HBM per device.

```python
import math
import jax
import jax.numpy as jnp
from jax import lax

D = 8192
HEAD_DIM = 128
HEADS = 32
KV_HEADS = 4
RANK = 64
SEQ = 128
NPROMPT = 64
TOKENS = 8192


def label_table(key):
    shuffled = jax.random.permutation(jax.random.fold_in(key, 7), NPROMPT)
    return (shuffled % 2).astype(jnp.int32)


def length_table(key):
    drawn = jax.random.randint(jax.random.fold_in(key, 3), (NPROMPT,), SEQ // 4, SEQ + 1)
    chosen = jax.random.randint(jax.random.fold_in(key, 5), (), 0, NPROMPT)
    return jnp.where(jnp.arange(NPROMPT) == chosen, SEQ, drawn).astype(jnp.int32)


def draw_labels(key, part):
    return label_table(key)


def draw_lengths(key, part):
    return length_table(key)


def draw_token_mask(key, part):
    prompt_lengths = length_table(key)
    coin_flips = jax.random.randint(jax.random.fold_in(key, 11), (NPROMPT, SEQ), 0, 2)
    position = jnp.arange(SEQ)[None, :]
    live_slot = position < prompt_lengths[:, None]
    last_slot = position == prompt_lengths[:, None] - 1
    marked = jnp.where(last_slot, 1, jnp.where(live_slot, coin_flips, 0))
    return marked.astype(jnp.int32).reshape(TOKENS)


def draw_hidden_states(key, part):
    prompt_labels = label_table(key)
    harmful = jnp.repeat(prompt_labels, SEQ).astype(jnp.float32)
    class_shift = jnp.clip(0.15 * jax.random.normal(jax.random.fold_in(key, 17), (D,), jnp.float32), -0.6, 0.6)
    noise_part = jnp.clip(jax.random.normal(jax.random.fold_in(key, 13), (TOKENS, D), jnp.float32), -6.0, 6.0)
    return (noise_part + harmful[:, None] * class_shift[None, :]).astype(jnp.bfloat16)


def shard_levels(own_key, shape, split, smallest, high):
    gain, own = 1.0, jax.random.fold_in(own_key, 6)
    for dim, blocks in split:
        draws = jnp.exp(jax.random.uniform(jax.random.fold_in(own, dim), (blocks,), jnp.float32, smallest / len(split), high / len(split)))
        gain = gain * jnp.repeat(draws, shape[dim] // blocks).reshape([-1 if axis == dim else 1 for axis in range(len(shape))])
    return gain


def gaussian(key, dims, spread, reach, pieces=(), dtype=jnp.bfloat16):
    values = jax.random.normal(key, dims, jnp.float32) * spread
    if len(pieces) > 0:
        values = shard_levels(key, dims, pieces, -0.22, 0.18) * values
    return jnp.clip(values, min=-reach, max=reach).astype(dtype)


def setup_inputs(seed: int = 0) -> dict:
    streams_of = jax.random.split(jax.random.key(seed), 13)
    return {
        "hidden_states": draw_hidden_states(jax.random.fold_in(streams_of[12], 71), 0),
        "lengths": draw_lengths(jax.random.fold_in(streams_of[12], 71), 0),
        "labels": draw_labels(jax.random.fold_in(streams_of[12], 71), 0),
        "token_mask": draw_token_mask(jax.random.fold_in(streams_of[12], 71), 0),
        "q_weight": gaussian(streams_of[4], (D, HEADS * HEAD_DIM), D ** -0.5, 0.0625, ((0, 32), (1, 16))),
        "k_weight": gaussian(streams_of[5], (D, KV_HEADS * HEAD_DIM), D ** -0.5, 0.0625, ((0, 32), (1, 16))),
        "v_weight": gaussian(streams_of[6], (D, KV_HEADS * HEAD_DIM), D ** -0.5, 0.0625, ((0, 32), (1, 16))),
        "q_down": gaussian(streams_of[7], (D, RANK), D ** -0.5, 0.0625, ((0, 32),)),
        "v_down": gaussian(streams_of[8], (D, RANK), D ** -0.5, 0.0625, ((0, 32),)),
        "query_up_weight": gaussian(streams_of[9], (RANK, HEADS * HEAD_DIM), 0.05, 0.29882812, ((1, 16),)),
        "value_up_weight": gaussian(streams_of[10], (RANK, KV_HEADS * HEAD_DIM), 0.05, 0.29882812, ((1, 16),)),
        "out_grad": gaussian(streams_of[11], (TOKENS, HEADS * HEAD_DIM), (8.0 * TOKENS ** -0.5), 0.52734375, ((0, 32), (1, 16))),
    }


ADAPTER_SCALE = 2.0
EPSILON = 1e-06

def reference(hidden_states, lengths, labels, token_mask, q_weight, k_weight, v_weight, q_down, v_down, query_up_weight, value_up_weight, out_grad):
    harmful = jnp.repeat(labels, SEQ).astype(jnp.float32)
    chosen = token_mask.astype(jnp.float32)
    class_rows = jnp.stack([chosen * harmful, chosen * (1.0 - harmful)]).astype(jnp.bfloat16)
    class_sums = jnp.dot(class_rows, hidden_states, preferred_element_type=jnp.float32)
    class_counts = lax.optimization_barrier(jnp.sum(class_rows.astype(jnp.float32), axis=1))
    difference = class_sums[0] / class_counts[0] - class_sums[1] / class_counts[1]
    direction = difference * lax.rsqrt(jnp.mean(difference * difference) + EPSILON) / math.sqrt(D)
    states = hidden_states.astype(jnp.float32)
    along = lax.optimization_barrier(jnp.sum(states * direction[None, :], axis=1))
    ablated = (states - (harmful * along)[:, None] * direction[None, :]).astype(jnp.bfloat16)
    query_frozen_output = jnp.dot(ablated, q_weight, preferred_element_type=jnp.float32)
    keys = jnp.dot(ablated, k_weight, preferred_element_type=jnp.float32).astype(jnp.bfloat16)
    value_frozen_output = jnp.dot(ablated, v_weight, preferred_element_type=jnp.float32)
    query_adapter_output = jnp.dot(ablated, q_down, preferred_element_type=jnp.float32).astype(jnp.bfloat16)
    value_adapter_output = jnp.dot(ablated, v_down, preferred_element_type=jnp.float32).astype(jnp.bfloat16)
    query_matrix = (query_frozen_output + ADAPTER_SCALE * jnp.dot(query_adapter_output, query_up_weight, preferred_element_type=jnp.float32)).astype(jnp.bfloat16)
    value_matrix = (value_frozen_output + ADAPTER_SCALE * jnp.dot(value_adapter_output, value_up_weight, preferred_element_type=jnp.float32)).astype(jnp.bfloat16)
    group_size = HEADS // KV_HEADS
    query_heads = query_matrix.reshape(NPROMPT, SEQ, HEADS, HEAD_DIM).astype(jnp.float32)
    key_split = jnp.transpose(keys.reshape(NPROMPT, SEQ, HEAD_DIM, KV_HEADS), (0, 1, 3, 2))
    value_split = jnp.transpose(value_matrix.reshape(NPROMPT, SEQ, HEAD_DIM, KV_HEADS), (0, 1, 3, 2))
    key_heads = jnp.repeat(key_split, group_size, axis=2).astype(jnp.float32)
    value_heads = jnp.repeat(value_split, group_size, axis=2).astype(jnp.float32)
    position = jnp.arange(SEQ)
    allowed = (position[None, None, :] <= position[None, :, None]) & (position[None, None, :] < lengths[:, None, None])
    scores = jnp.einsum('pshd,pthd->phst', query_heads, key_heads) / math.sqrt(HEAD_DIM)
    masked = jnp.where(allowed[:, None], scores, -1e+30)
    row_peak = lax.optimization_barrier(jnp.max(masked, axis=-1, keepdims=True))
    exponent = jnp.where(allowed[:, None], jnp.exp(masked - row_peak), 0.0)
    probs = exponent / lax.optimization_barrier(jnp.sum(exponent, axis=-1, keepdims=True))
    probs_low = probs.astype(jnp.bfloat16)
    attended = jnp.einsum('phst,pthd->pshd', probs_low.astype(jnp.float32), value_heads)
    valid = (position[None, :] < lengths[:, None]).astype(jnp.bfloat16)
    live_grad = out_grad.reshape(NPROMPT, SEQ, HEADS, HEAD_DIM) * valid[:, :, None, None]
    live_float = live_grad.astype(jnp.float32)
    row_terms = lax.optimization_barrier(jnp.sum(live_float * attended, axis=-1))
    prob_grad = jnp.einsum('pshd,pthd->phst', live_float, value_heads)
    score_grad = (probs * (prob_grad - jnp.transpose(row_terms, (0, 2, 1))[..., None])).astype(jnp.bfloat16)
    query_gradient = (jnp.einsum('phst,pthd->pshd', score_grad.astype(jnp.float32), key_heads) / math.sqrt(HEAD_DIM)).astype(jnp.bfloat16)
    query_gradient = query_gradient.reshape(TOKENS, HEADS * HEAD_DIM)
    value_heads_grad = jnp.einsum('phst,pshd->pthd', probs_low.astype(jnp.float32), live_float)
    value_gradient = lax.optimization_barrier(jnp.sum(value_heads_grad.reshape(NPROMPT, SEQ, KV_HEADS, group_size, HEAD_DIM), axis=3))
    value_gradient = jnp.transpose(value_gradient, (0, 1, 3, 2)).reshape(TOKENS, KV_HEADS * HEAD_DIM).astype(jnp.bfloat16)
    query_up_gradient = ADAPTER_SCALE * jnp.dot(query_adapter_output.T, query_gradient, preferred_element_type=jnp.float32)
    value_up_gradient = ADAPTER_SCALE * jnp.dot(value_adapter_output.T, value_gradient, preferred_element_type=jnp.float32)
    query_backward = (ADAPTER_SCALE * jnp.dot(query_gradient, query_up_weight.T, preferred_element_type=jnp.float32)).astype(jnp.bfloat16)
    value_backward = (ADAPTER_SCALE * jnp.dot(value_gradient, value_up_weight.T, preferred_element_type=jnp.float32)).astype(jnp.bfloat16)
    q_down_grad = jnp.dot(ablated.T, query_backward, preferred_element_type=jnp.float32)
    v_down_grad = jnp.dot(ablated.T, value_backward, preferred_element_type=jnp.float32)
    return (q_down_grad, v_down_grad, query_up_gradient, value_up_gradient)
```

```python
import functools
import math

import jax
import jax.numpy as jnp
from jax import lax
from jax.experimental import pallas as pl
from jax.experimental.pallas import tpu as pltpu
from jax.sharding import PartitionSpec as P

HEAD_DIM = 128
HEADS = 32
KV_HEADS = 4
SEQ = 128
RANK = 64
ADAPTER_SCALE = 2.0
EPSILON = 1e-06
MESH = pl.DeviceIdType.MESH
F32 = jnp.float32
BF16 = jnp.bfloat16


def dot(a, b, ca, cb):
    return lax.dot_general(a, b, (((ca,), (cb,)), ((), ())), preferred_element_type=F32)


def exchange_kernel(axis, n, picks, finish, *refs):
    count = len(picks)
    xs, rest = refs[:count], refs[count:]
    recvs, rest = rest[-count - 2 : -2], (rest[: -count - 2], rest[-2], rest[-1])
    outs, send_sem, recv_sem = rest
    me = lax.axis_index(axis)
    barrier = pltpu.get_barrier_semaphore()

    def greet(k, carry):
        peer = lax.rem(me + k, n)
        pl.semaphore_signal(barrier, inc=1, device_id={axis: peer}, device_id_type=MESH)
        return carry

    lax.fori_loop(1, n, greet, 0)
    pl.semaphore_wait(barrier, n - 1)

    def piece(a, peer):
        return xs[a] if picks[a] is None else xs[a].at[picks[a](peer)]

    def copy(a, k):
        peer = lax.rem(me + k, n)
        return pltpu.make_async_remote_copy(
            src_ref=piece(a, peer),
            dst_ref=recvs[a].at[me],
            send_sem=send_sem.at[a, peer],
            recv_sem=recv_sem.at[a, me],
            device_id={axis: peer},
            device_id_type=MESH,
        )

    def arrival(a, k):
        peer = lax.rem(me + k, n)
        return pltpu.make_async_remote_copy(
            src_ref=piece(a, peer),
            dst_ref=recvs[a].at[peer],
            send_sem=send_sem.at[a, peer],
            recv_sem=recv_sem.at[a, peer],
            device_id={axis: peer},
            device_id_type=MESH,
        )

    def send(k, carry):
        for a in range(count):
            copy(a, k).start()
        return carry

    lax.fori_loop(1, n, send, 0)
    for a in range(count):
        recvs[a][me] = xs[a][...] if picks[a] is None else xs[a][picks[a](me)]

    def take(k, carry):
        for a in range(count):
            arrival(a, k).wait()
        return carry

    lax.fori_loop(1, n, take, 0)
    finish(recvs, outs)


def exchange(axis, n, arrays, picks, finish, out_shape, cid):
    count = len(arrays)
    shapes = [x.shape if p is None else x.shape[1:] for x, p in zip(arrays, picks)]
    vmem = pl.BlockSpec(memory_space=pltpu.VMEM)
    return pl.pallas_call(
        functools.partial(exchange_kernel, axis, n, picks, finish),
        out_shape=out_shape,
        in_specs=[vmem] * count,
        out_specs=[vmem] * len(out_shape),
        scratch_shapes=[
            *[pltpu.VMEM((n, *s), x.dtype) for s, x in zip(shapes, arrays)],
            pltpu.SemaphoreType.DMA((count, n)),
            pltpu.SemaphoreType.DMA((count, n)),
        ],
        compiler_params=pltpu.CompilerParams(collective_id=cid, has_side_effects=True),
    )(*arrays)


def total(ref, n):
    acc = ref[0]
    for k in range(1, n):
        acc = acc + ref[k]
    return acc


def finish_class(recvs, outs):
    s = total(recvs[0], recvs[0].shape[0])
    outs[0][...] = s[0:4] / s[8:9] - s[4:8] / s[9:10]


def finish_plain(recvs, outs):
    for r, o in zip(recvs, outs):
        o[...] = r[...]


def finish_value(recvs, outs):
    per = recvs[0].shape[0] // KV_HEADS
    for g in range(KV_HEADS):
        acc = recvs[0][per * g]
        for k in range(1, per):
            acc = acc + recvs[0][per * g + k]
        outs[0][g] = acc


def finish_total(recvs, outs):
    for r, o in zip(recvs, outs):
        o[...] = total(r, r.shape[0])


def attention_kernel(
    lengths, base, low, up, keys, values, og, qgrad_out, value_out, upgrad_out, back_out
):
    query_low = low[0:RANK, :]
    query = (base[...] + ADAPTER_SCALE * dot(query_low, up[...], 0, 0)).astype(BF16)
    prompts = base.shape[0] // SEQ
    heads = base.shape[1] // HEAD_DIM
    row = lax.broadcasted_iota(jnp.int32, (SEQ, SEQ), 0)
    col = lax.broadcasted_iota(jnp.int32, (SEQ, SEQ), 1)
    scale = 1.0 / math.sqrt(HEAD_DIM)
    for p in range(prompts):
        length = lengths[p]
        allowed = (col <= row) & (col < length)
        ts = slice(p * SEQ, (p + 1) * SEQ)
        kt = keys[:, ts]
        vt = values[:, ts]
        vsum = None
        for h in range(heads):
            hs = slice(h * HEAD_DIM, (h + 1) * HEAD_DIM)
            scores = dot(query[ts, hs], kt, 1, 0) * scale
            masked = jnp.where(allowed, scores, -1e30)
            peak = jnp.max(masked, axis=1, keepdims=True)
            expo = jnp.where(allowed, jnp.exp(masked - peak), 0.0)
            probs = expo / jnp.sum(expo, axis=1, keepdims=True)
            probs_low = probs.astype(BF16)
            attended = dot(probs_low, vt, 1, 1)
            live32 = jnp.where(row < length, og[ts, hs].astype(F32), 0.0)
            live = live32.astype(BF16)
            terms = jnp.sum(live32 * attended, axis=1, keepdims=True)
            pgrad = dot(live, vt, 1, 0)
            sgrad = (probs * (pgrad - terms)).astype(BF16)
            qgrad_out[ts, hs] = (dot(sgrad, kt, 1, 1) * scale).astype(BF16)
            part = dot(live, probs_low, 0, 0)
            vsum = part if vsum is None else vsum + part
        value_out[:, ts] = vsum
    qg = qgrad_out[...]
    upgrad_out[...] = ADAPTER_SCALE * dot(query_low, qg, 1, 0)
    back_out[...] = ADAPTER_SCALE * dot(up[...], qg, 1, 1)


def attention(lengths, base, low, up, keys, values, og):
    tok, cols = base.shape
    vmem = pl.BlockSpec(memory_space=pltpu.VMEM)
    return pl.pallas_call(
        attention_kernel,
        out_shape=(
            jax.ShapeDtypeStruct((tok, cols), BF16),
            jax.ShapeDtypeStruct((HEAD_DIM, tok), F32),
            jax.ShapeDtypeStruct((RANK, cols), F32),
            jax.ShapeDtypeStruct((RANK, tok), F32),
        ),
        in_specs=[pl.BlockSpec(memory_space=pltpu.SMEM)] + [vmem] * 6,
        out_specs=[vmem] * 4,
    )(lengths, base, low, up, keys, values, og)


def body(
    dp,
    fsdp,
    hidden_states,
    lengths,
    labels,
    token_mask,
    q_weight,
    k_weight,
    v_weight,
    q_down,
    v_down,
    query_up_weight,
    value_up_weight,
    out_grad,
):
    tok, width = hidden_states.shape
    j = lax.axis_index("fsdp")
    rows = q_weight.shape[0]
    qc, kc = q_weight.shape[1], k_weight.shape[1]
    dk = kc // KV_HEADS
    rk = 2 * RANK // fsdp
    per_group = fsdp // KV_HEADS
    group = lambda peer: peer // per_group

    downs = jnp.concatenate([q_down, v_down], axis=1)
    my_down = lax.dynamic_slice(downs, (0, j * rk), (rows, rk))
    pad = 128 - 2 * kc - rk
    packed = jnp.concatenate(
        [q_weight, k_weight, v_weight, my_down, jnp.zeros((rows, pad), BF16)], axis=1
    )
    weights = lax.all_gather(packed, "dp", axis=0, tiled=True)

    harmful = jnp.repeat(labels, SEQ).astype(F32)
    chosen = token_mask.astype(F32)
    class_rows = jnp.stack([chosen * harmful, chosen * (1.0 - harmful)])
    counts = jnp.sum(class_rows, axis=1)
    share = width // fsdp
    mine = lax.dynamic_slice(hidden_states, (0, j * share), (tok, share))
    sums = jnp.dot(class_rows.astype(BF16), mine, preferred_element_type=F32)
    sums = jnp.concatenate(
        [
            sums.reshape(8, 128),
            jnp.broadcast_to(counts[:, None], (2, 128)),
            jnp.zeros((6, 128), F32),
        ],
        axis=0,
    )
    (diff_part,) = exchange(
        "dp", dp, [sums], [None], finish_class, [jax.ShapeDtypeStruct((4, 128), F32)], 1
    )
    vup = value_up_weight.reshape(RANK, dk, KV_HEADS).transpose(2, 1, 0)
    vup_piece = jnp.pad(vup.astype(F32), ((0, 0), (0, 0), (0, 128 - RANK)))
    diff_tile = jnp.concatenate([diff_part, jnp.zeros((4, 128), F32)], axis=0)
    diff_all, vup_all = exchange(
        "fsdp",
        fsdp,
        [diff_tile, vup_piece],
        [None, group],
        finish_plain,
        [
            jax.ShapeDtypeStruct((fsdp, 8, 128), F32),
            jax.ShapeDtypeStruct((fsdp, dk, 128), F32),
        ],
        2,
    )
    difference = diff_all[:, :4].reshape(width)
    vup_head = vup_all[:, :, :RANK].reshape(HEAD_DIM, RANK).astype(BF16)
    direction = (
        difference * lax.rsqrt(jnp.mean(difference * difference) + EPSILON) / math.sqrt(width)
    )
    states = hidden_states.astype(F32)
    along = jnp.sum(states * direction[None, :], axis=1)
    ablated = (states - (harmful * along)[:, None] * direction[None, :]).astype(BF16)

    projected = jnp.dot(ablated, weights, preferred_element_type=F32)
    base = projected[:, :qc]
    small = projected[:, qc : qc + 2 * kc + rk].T
    key_part = small[:kc].reshape(dk, KV_HEADS, tok).transpose(1, 0, 2).astype(BF16)
    value_part = small[kc : 2 * kc].reshape(dk, KV_HEADS, tok).transpose(1, 0, 2)
    top = lax.reduce_precision(value_part, 8, 7)
    high = top.astype(BF16)
    rest = (value_part - top).astype(BF16)
    low_part = jnp.broadcast_to(small[2 * kc :].astype(BF16)[None], (KV_HEADS, rk, tok))
    pieces = jnp.concatenate([key_part, high, rest, low_part], axis=1)
    (got,) = exchange(
        "fsdp",
        fsdp,
        [pieces],
        [group],
        finish_plain,
        [jax.ShapeDtypeStruct((fsdp, *pieces.shape[1:]), BF16)],
        3,
    )
    keys = got[:, :dk].reshape(HEAD_DIM, tok)
    value_base = got[:, dk : 2 * dk].astype(F32) + got[:, 2 * dk : 3 * dk].astype(F32)
    low = got[:, 3 * dk :].reshape(2 * RANK, tok)
    values = (
        value_base.reshape(HEAD_DIM, tok) + ADAPTER_SCALE * dot(vup_head, low[RANK:], 1, 0)
    ).astype(BF16)

    _, vgrad_part, qup_part, qback = attention(
        lengths, base, low, query_up_weight, keys, values, out_grad
    )
    (vgrad,) = exchange(
        "fsdp",
        fsdp,
        [vgrad_part.reshape(fsdp, dk, tok)],
        [lambda peer: peer],
        finish_value,
        [jax.ShapeDtypeStruct((KV_HEADS, dk, tok), F32)],
        4,
    )
    vgrad = vgrad.reshape(kc, tok).astype(BF16)
    vback = ADAPTER_SCALE * dot(vup.reshape(kc, RANK), vgrad, 0, 0)
    vup_part = ADAPTER_SCALE * dot(low[RANK:], vgrad, 1, 1)
    vup_part = vup_part.reshape(RANK, KV_HEADS, dk).transpose(0, 2, 1).reshape(RANK, kc)
    (back,) = exchange(
        "fsdp",
        fsdp,
        [jnp.concatenate([qback, vback], axis=0).reshape(fsdp, rk, tok)],
        [lambda peer: peer],
        finish_total,
        [jax.ShapeDtypeStruct((rk, tok), F32)],
        5,
    )
    down_part = jnp.dot(back.astype(BF16), ablated, preferred_element_type=F32)
    down_part = down_part.reshape(rk, dp, rows).transpose(1, 0, 2)
    ur = RANK // dp
    ups = jnp.concatenate(
        [qup_part.reshape(dp, ur * qc), vup_part.reshape(dp, ur * kc)], axis=1
    )
    fill = -ups.shape[1] % 1024
    ups = jnp.pad(ups, ((0, 0), (0, fill))).reshape(dp, -1, 128)
    down_mine, up_mine = exchange(
        "dp",
        dp,
        [down_part, ups],
        [lambda peer: peer] * 2,
        finish_total,
        [
            jax.ShapeDtypeStruct((rk, rows), F32),
            jax.ShapeDtypeStruct(ups.shape[1:], F32),
        ],
        6,
    )
    (downs_all,) = exchange(
        "fsdp",
        fsdp,
        [down_mine],
        [None],
        finish_plain,
        [jax.ShapeDtypeStruct((fsdp, rk, rows), F32)],
        7,
    )
    down_grad = downs_all.reshape(2 * RANK, rows).T
    up_flat = up_mine.reshape(-1)
    return (
        down_grad[:, :RANK],
        down_grad[:, RANK:],
        up_flat[: ur * qc].reshape(ur, qc),
        up_flat[ur * qc : ur * (qc + kc)].reshape(ur, kc),
    )


def solution(mesh):
    placed = (
        P("dp", None),
        P("dp"),
        P("dp"),
        P("dp"),
        P("dp", "fsdp"),
        P("dp", "fsdp"),
        P("dp", "fsdp"),
        P("dp", None),
        P("dp", None),
        P(None, "fsdp"),
        P(None, "fsdp"),
        P("dp", "fsdp"),
    )
    return jax.shard_map(
        functools.partial(body, mesh.shape["dp"], mesh.shape["fsdp"]),
        mesh=mesh,
        in_specs=placed,
        out_specs=(P("dp", None), P("dp", None), P("dp", "fsdp"), P("dp", "fsdp")),
        check_vma=False,
    )
```

```python
import functools
import math

import jax
import jax.numpy as jnp
from jax import lax
from jax.experimental import pallas as pl
from jax.experimental.pallas import tpu as pltpu
from jax.sharding import PartitionSpec as P

HEAD_DIM = 128
HEADS = 32
KV_HEADS = 4
SEQ = 128
RANK = 64
ADAPTER_SCALE = 2.0
EPSILON = 1e-06
MESH = pl.DeviceIdType.MESH
F32 = jnp.float32
BF16 = jnp.bfloat16


def dot(a, b, ca, cb):
    return lax.dot_general(a, b, (((ca,), (cb,)), ((), ())), preferred_element_type=F32)


def exchange_kernel(axis, n, picks, finish, *refs):
    count = len(picks)
    xs, rest = refs[:count], refs[count:]
    recvs, rest = rest[-count - 2 : -2], (rest[: -count - 2], rest[-2], rest[-1])
    outs, send_sem, recv_sem = rest
    me = lax.axis_index(axis)
    barrier = pltpu.get_barrier_semaphore()

    def greet(k, carry):
        peer = lax.rem(me + k, n)
        pl.semaphore_signal(barrier, inc=1, device_id={axis: peer}, device_id_type=MESH)
        return carry

    lax.fori_loop(1, n, greet, 0)
    pl.semaphore_wait(barrier, n - 1)

    def piece(a, peer):
        return xs[a] if picks[a] is None else xs[a].at[picks[a](peer)]

    def copy(a, k):
        peer = lax.rem(me + k, n)
        return pltpu.make_async_remote_copy(
            src_ref=piece(a, peer),
            dst_ref=recvs[a].at[me],
            send_sem=send_sem.at[a, peer],
            recv_sem=recv_sem.at[a, me],
            device_id={axis: peer},
            device_id_type=MESH,
        )

    def arrival(a, k):
        peer = lax.rem(me + k, n)
        return pltpu.make_async_remote_copy(
            src_ref=piece(a, peer),
            dst_ref=recvs[a].at[peer],
            send_sem=send_sem.at[a, peer],
            recv_sem=recv_sem.at[a, peer],
            device_id={axis: peer},
            device_id_type=MESH,
        )

    def send(k, carry):
        for a in range(count):
            copy(a, k).start()
        return carry

    lax.fori_loop(1, n, send, 0)
    for a in range(count):
        recvs[a][me] = xs[a][...] if picks[a] is None else xs[a][picks[a](me)]

    def take(k, carry):
        for a in range(count):
            arrival(a, k).wait()
        return carry

    lax.fori_loop(1, n, take, 0)
    finish(recvs, outs)


def exchange(axis, n, arrays, picks, finish, out_shape, cid):
    count = len(arrays)
    shapes = [x.shape if p is None else x.shape[1:] for x, p in zip(arrays, picks)]
    vmem = pl.BlockSpec(memory_space=pltpu.VMEM)
    return pl.pallas_call(
        functools.partial(exchange_kernel, axis, n, picks, finish),
        out_shape=out_shape,
        in_specs=[vmem] * count,
        out_specs=[vmem] * len(out_shape),
        scratch_shapes=[
            *[pltpu.VMEM((n, *s), x.dtype) for s, x in zip(shapes, arrays)],
            pltpu.SemaphoreType.DMA((count, n)),
            pltpu.SemaphoreType.DMA((count, n)),
        ],
        compiler_params=pltpu.CompilerParams(collective_id=cid, has_side_effects=True),
    )(*arrays)


def total(ref, n):
    acc = ref[0]
    for k in range(1, n):
        acc = acc + ref[k]
    return acc


def finish_plain(recvs, outs):
    for r, o in zip(recvs, outs):
        o[...] = r[...]


def finish_value(recvs, outs):
    per = recvs[0].shape[0] // KV_HEADS
    for g in range(KV_HEADS):
        acc = recvs[0][per * g]
        for k in range(1, per):
            acc = acc + recvs[0][per * g + k]
        outs[0][g] = acc


def finish_total(recvs, outs):
    for r, o in zip(recvs, outs):
        o[...] = total(r, r.shape[0])


def attention_kernel(
    lengths, base, low, up, keys, values, og, qgrad_out, value_out, upgrad_out, back_out
):
    query_low = low[0:RANK, :]
    query = (base[...] + ADAPTER_SCALE * dot(query_low, up[...], 0, 0)).astype(BF16)
    prompts = base.shape[0] // SEQ
    heads = base.shape[1] // HEAD_DIM
    row = lax.broadcasted_iota(jnp.int32, (SEQ, SEQ), 0)
    col = lax.broadcasted_iota(jnp.int32, (SEQ, SEQ), 1)
    scale = 1.0 / math.sqrt(HEAD_DIM)
    for p in range(prompts):
        length = lengths[p]
        allowed = (col <= row) & (col < length)
        ts = slice(p * SEQ, (p + 1) * SEQ)
        kt = keys[:, ts]
        vt = values[:, ts]
        vsum = None
        for h in range(heads):
            hs = slice(h * HEAD_DIM, (h + 1) * HEAD_DIM)
            scores = dot(query[ts, hs], kt, 1, 0) * scale
            masked = jnp.where(allowed, scores, -1e30)
            peak = jnp.max(masked, axis=1, keepdims=True)
            expo = jnp.where(allowed, jnp.exp(masked - peak), 0.0)
            probs = expo / jnp.sum(expo, axis=1, keepdims=True)
            probs_low = probs.astype(BF16)
            attended = dot(probs_low, vt, 1, 1)
            live32 = jnp.where(row < length, og[ts, hs].astype(F32), 0.0)
            live = live32.astype(BF16)
            terms = jnp.sum(live32 * attended, axis=1, keepdims=True)
            pgrad = dot(live, vt, 1, 0)
            sgrad = (probs * (pgrad - terms)).astype(BF16)
            qgrad_out[ts, hs] = (dot(sgrad, kt, 1, 1) * scale).astype(BF16)
            part = dot(live, probs_low, 0, 0)
            vsum = part if vsum is None else vsum + part
        value_out[:, ts] = vsum
    qg = qgrad_out[...]
    upgrad_out[...] = ADAPTER_SCALE * dot(query_low, qg, 1, 0)
    back_out[...] = ADAPTER_SCALE * dot(up[...], qg, 1, 1)


def attention(lengths, base, low, up, keys, values, og):
    tok, cols = base.shape
    vmem = pl.BlockSpec(memory_space=pltpu.VMEM)
    return pl.pallas_call(
        attention_kernel,
        out_shape=(
            jax.ShapeDtypeStruct((tok, cols), BF16),
            jax.ShapeDtypeStruct((HEAD_DIM, tok), F32),
            jax.ShapeDtypeStruct((RANK, cols), F32),
            jax.ShapeDtypeStruct((RANK, tok), F32),
        ),
        in_specs=[pl.BlockSpec(memory_space=pltpu.SMEM)] + [vmem] * 6,
        out_specs=[vmem] * 4,
    )(lengths, base, low, up, keys, values, og)


XS = 4
SPLIT = 144


def gather_kernel(
    dp, fsdp, hidden, class_rows, harm, block, vup, base_out, small_out, ablated_out, vup_out,
    buf, sums, sums_all, diff, diff_all, vup_all, dirs, own_sem, send_sem, recv_sem,
    sums_send, sums_recv, diff_send, diff_recv, vup_send, vup_recv,
):
    me = lax.axis_index("dp")
    j = lax.axis_index("fsdp")
    zs = dp // XS
    z, x = me // XS, me % XS
    tok, width = hidden.shape
    rows, cols = buf.shape[1], buf.shape[2]
    share = width // fsdp
    tiles = share // 128
    per_group = fsdp // KV_HEADS
    barrier = pltpu.get_barrier_semaphore()

    def greet(axis, i, n):
        def step(k, carry):
            peer = lax.rem(i + k, n)
            pl.semaphore_signal(barrier, inc=1, device_id={axis: peer}, device_id_type=MESH)
            return carry

        lax.fori_loop(1, n, step, 0)

    greet("dp", me, dp)
    greet("fsdp", j, fsdp)
    own = pltpu.make_async_copy(block, buf.at[me], own_sem)
    own.start()
    cr = class_rows[...]
    part = dot(cr, hidden[:, pl.ds(pl.multiple_of(j * share, share), share)], 1, 0)
    counts = jnp.sum(cr.astype(F32), axis=1, keepdims=True)
    sums[...] = jnp.zeros_like(sums)
    for g in range(2):
        for c in range(tiles):
            r = g * tiles + c
            sums[r : r + 1, :] = part[g : g + 1, c * 128 : (c + 1) * 128]
        sums[8 + g : 9 + g, :] = jnp.broadcast_to(counts[g : g + 1, :], (1, 128))
    pl.semaphore_wait(barrier, dp + fsdp - 2)

    def direct(axis, i, n, src, dst, send, recv):
        def copy(k, slot):
            peer = lax.rem(i + k, n)
            return pltpu.make_async_remote_copy(
                src_ref=src(peer),
                dst_ref=dst.at[i if slot is None else peer],
                send_sem=send.at[peer],
                recv_sem=recv.at[i if slot is None else peer],
                device_id={axis: peer},
                device_id_type=MESH,
            )

        def start(k, carry):
            copy(k, None).start()
            return carry

        def finish(k, carry):
            copy(k, 0).wait()
            return carry

        return (
            lambda: lax.fori_loop(1, n, start, 0),
            lambda: lax.fori_loop(1, n, finish, 0),
        )

    sums_start, sums_wait = direct(
        "dp", me, dp, lambda peer: sums, sums_all, sums_send, sums_recv
    )
    diff_start, diff_wait = direct(
        "fsdp", j, fsdp, lambda peer: diff, diff_all, diff_send, diff_recv
    )
    vup_start, vup_wait = direct(
        "fsdp", j, fsdp, lambda peer: vup.at[peer // per_group], vup_all, vup_send, vup_recv
    )
    sums_start()

    span = (pl.ds(0, SPLIT), pl.ds(SPLIT, rows - SPLIT))
    sent = []

    def place(dz, dx):
        return lax.rem(z + dz + zs, zs) * XS + lax.rem(x + dx, XS)

    def push(half, origin, target, mine=False):
        there = buf.at[origin, span[half]]
        c = pltpu.make_async_remote_copy(
            src_ref=block.at[span[half]] if mine else there,
            dst_ref=there,
            send_sem=send_sem.at[len(sent)],
            recv_sem=recv_sem.at[half, origin],
            device_id={"dp": target},
            device_id_type=MESH,
        )
        c.start()
        sent.append(c)

    def landed(half, origin):
        there = buf.at[origin, span[half]]
        pltpu.make_async_remote_copy(
            src_ref=there,
            dst_ref=there,
            send_sem=send_sem.at[0],
            recv_sem=recv_sem.at[half, origin],
            device_id={"dp": place(1, 0)},
            device_id_type=MESH,
        ).wait_recv()

    reach = ((4, 3), (3, 4))
    up, down = place(1, 0), place(-1, 0)
    for half in (0, 1):
        push(half, me, up, True)
        push(half, me, down, True)
    for half in (0, 1):
        for dx in range(1, XS):
            push(half, me, place(0, dx), True)
    vup_start()
    for dx in range(1, XS):
        origin = place(0, dx)
        landed(0, origin)
        push(0, origin, up)
        push(0, origin, down)

    def forward(k):
        for side, sign, target in ((0, -1, up), (1, 1, down)):
            if k <= reach[1][side]:
                origin = place(sign * k, 0)
                landed(1, origin)
                if k < reach[1][side]:
                    push(1, origin, target)
                for dx in range(1, XS):
                    push(1, origin, place(0, dx))
            if k <= reach[0][side]:
                for dx in range(XS):
                    origin = place(sign * k, dx)
                    landed(0, origin)
                    if k < reach[0][side]:
                        push(0, origin, target)

    def multiply(k):
        for dz in sorted({-k, k} if k < zs // 2 else {k}):
            for dx in range(1, XS):
                landed(1, place(dz, dx))
            first = place(dz, 0) - x

            def step(i, carry):
                origin = first + i
                lanes = pl.ds(pl.multiple_of(origin * cols, cols), cols)
                a = ablated_out[:, lanes]
                base_out[...] += dot(a, buf[origin, 0:cols, :], 1, 0)
                small_out[...] += dot(buf[origin, cols:rows, :], a, 1, 1)
                return carry

            lax.fori_loop(0, XS, step, 0)

    sums_all[me] = sums[...]
    sums_wait()
    t = total(sums_all, dp)
    diff[...] = jnp.zeros_like(diff)
    diff[0:tiles] = t[0:tiles] / t[8:9] - t[tiles : 2 * tiles] / t[9:10]
    forward(1)
    diff_start()
    diff_all[j] = diff[...]
    vup_all[j] = vup[j // per_group]
    base_out[...] = jnp.zeros_like(base_out)
    small_out[...] = jnp.zeros_like(small_out)
    diff_wait()
    d = diff_all[...]
    square = jnp.sum(jnp.sum(jnp.sum(d * d, axis=0), axis=0, keepdims=True), axis=1, keepdims=True)
    scale = lax.rsqrt(square / width + EPSILON) / math.sqrt(width)
    dirs[...] = d * scale

    def tile(c):
        return pl.ds(pl.multiple_of(c * 128, 128), 128)

    def project(b, acc):
        for i in range(tiles):
            c = b * tiles + i
            acc = acc + hidden[:, tile(c)].astype(F32) * dirs[b, i : i + 1, :]
        return acc

    acc = lax.fori_loop(0, fsdp, project, jnp.zeros((tok, 128), F32))
    along = harm[...] * jnp.sum(acc, axis=1, keepdims=True)

    def remove(b, carry):
        for i in range(tiles):
            c = b * tiles + i
            h = hidden[:, tile(c)].astype(F32)
            ablated_out[:, tile(c)] = (h - along * dirs[b, i : i + 1, :]).astype(BF16)
        return carry

    forward(2)
    lax.fori_loop(0, fsdp, remove, 0)
    forward(3)
    own.wait()
    multiply(0)
    multiply(1)
    forward(4)
    multiply(2)
    multiply(3)
    multiply(4)
    vup_wait()
    vup_out[...] = vup_all[...]
    for c in sent:
        c.wait_send()


def gather(dp, fsdp, hidden, class_rows, harm, block, vup):
    tok, width = hidden.shape
    rows, cols = block.shape
    vmem = pl.BlockSpec(memory_space=pltpu.VMEM)
    dma = pltpu.SemaphoreType.DMA
    return pl.pallas_call(
        functools.partial(gather_kernel, dp, fsdp),
        out_shape=(
            jax.ShapeDtypeStruct((tok, cols), F32),
            jax.ShapeDtypeStruct((rows - cols, tok), F32),
            jax.ShapeDtypeStruct((tok, width), BF16),
            jax.ShapeDtypeStruct((fsdp, *vup.shape[1:]), F32),
        ),
        in_specs=[vmem] * 5,
        out_specs=[vmem] * 4,
        scratch_shapes=[
            pltpu.VMEM((dp, rows, cols), BF16),
            pltpu.VMEM((16, 128), F32),
            pltpu.VMEM((dp, 16, 128), F32),
            pltpu.VMEM((8, 128), F32),
            pltpu.VMEM((fsdp, 8, 128), F32),
            pltpu.VMEM((fsdp, *vup.shape[1:]), F32),
            pltpu.VMEM((fsdp, 8, 128), F32),
            dma,
            dma((72,)),
            dma((2, dp)),
            dma((dp,)),
            dma((dp,)),
            dma((fsdp,)),
            dma((fsdp,)),
            dma((fsdp,)),
            dma((fsdp,)),
        ],
        compiler_params=pltpu.CompilerParams(
            collective_id=1, has_side_effects=True, vmem_limit_bytes=48 * 1024 * 1024
        ),
    )(hidden, class_rows, harm, block, vup)


def body(
    dp,
    fsdp,
    hidden_states,
    lengths,
    labels,
    token_mask,
    q_weight,
    k_weight,
    v_weight,
    q_down,
    v_down,
    query_up_weight,
    value_up_weight,
    out_grad,
):
    tok, width = hidden_states.shape
    j = lax.axis_index("fsdp")
    rows = q_weight.shape[0]
    qc, kc = q_weight.shape[1], k_weight.shape[1]
    dk = kc // KV_HEADS
    rk = 2 * RANK // fsdp
    per_group = fsdp // KV_HEADS
    group = lambda peer: peer // per_group

    downs = jnp.concatenate([q_down, v_down], axis=1)
    my_down = lax.dynamic_slice(downs, (0, j * rk), (rows, rk))
    lower = jnp.concatenate([k_weight, v_weight, my_down], axis=1).T
    lower = jnp.pad(lower, ((0, -lower.shape[0] % 16), (0, 0)))
    block = jnp.concatenate([q_weight, lower], axis=0)

    harmful = jnp.repeat(labels, SEQ).astype(F32)
    chosen = token_mask.astype(F32)
    class_rows = jnp.stack([chosen * harmful, chosen * (1.0 - harmful)])
    class_rows = jnp.pad(class_rows, ((0, 14), (0, 0))).astype(BF16)
    vup = value_up_weight.reshape(RANK, dk, KV_HEADS).transpose(2, 1, 0)
    vup_piece = jnp.pad(vup.astype(F32), ((0, 0), (0, 0), (0, 128 - RANK)))
    base, small, ablated, vup_all = gather(
        dp, fsdp, hidden_states, class_rows, harmful[:, None], block, vup_piece
    )
    vup_head = vup_all[:, :, :RANK].reshape(HEAD_DIM, RANK).astype(BF16)

    key_part = small[:kc].reshape(dk, KV_HEADS, tok).transpose(1, 0, 2).astype(BF16)
    value_part = small[kc : 2 * kc].reshape(dk, KV_HEADS, tok).transpose(1, 0, 2)
    top = lax.reduce_precision(value_part, 8, 7)
    high = top.astype(BF16)
    rest = (value_part - top).astype(BF16)
    low_part = jnp.broadcast_to(small[2 * kc : 2 * kc + rk].astype(BF16)[None], (KV_HEADS, rk, tok))
    pieces = jnp.concatenate([key_part, high, rest, low_part], axis=1)
    (got,) = exchange(
        "fsdp",
        fsdp,
        [pieces],
        [group],
        finish_plain,
        [jax.ShapeDtypeStruct((fsdp, *pieces.shape[1:]), BF16)],
        3,
    )
    keys = got[:, :dk].reshape(HEAD_DIM, tok)
    value_base = got[:, dk : 2 * dk].astype(F32) + got[:, 2 * dk : 3 * dk].astype(F32)
    low = got[:, 3 * dk :].reshape(2 * RANK, tok)
    values = (
        value_base.reshape(HEAD_DIM, tok) + ADAPTER_SCALE * dot(vup_head, low[RANK:], 1, 0)
    ).astype(BF16)

    _, vgrad_part, qup_part, qback = attention(
        lengths, base, low, query_up_weight, keys, values, out_grad
    )
    (vgrad,) = exchange(
        "fsdp",
        fsdp,
        [vgrad_part.reshape(fsdp, dk, tok)],
        [lambda peer: peer],
        finish_value,
        [jax.ShapeDtypeStruct((KV_HEADS, dk, tok), F32)],
        4,
    )
    vgrad = vgrad.reshape(kc, tok).astype(BF16)
    vback = ADAPTER_SCALE * dot(vup.reshape(kc, RANK), vgrad, 0, 0)
    vup_part = ADAPTER_SCALE * dot(low[RANK:], vgrad, 1, 1)
    vup_part = vup_part.reshape(RANK, KV_HEADS, dk).transpose(0, 2, 1).reshape(RANK, kc)
    (back,) = exchange(
        "fsdp",
        fsdp,
        [jnp.concatenate([qback, vback], axis=0).reshape(fsdp, rk, tok)],
        [lambda peer: peer],
        finish_total,
        [jax.ShapeDtypeStruct((rk, tok), F32)],
        5,
    )
    down_part = jnp.dot(back.astype(BF16), ablated, preferred_element_type=F32)
    down_part = down_part.reshape(rk, dp, rows).transpose(1, 0, 2)
    ur = RANK // dp
    ups = jnp.concatenate(
        [qup_part.reshape(dp, ur * qc), vup_part.reshape(dp, ur * kc)], axis=1
    )
    fill = -ups.shape[1] % 1024
    ups = jnp.pad(ups, ((0, 0), (0, fill))).reshape(dp, -1, 128)
    down_mine, up_mine = exchange(
        "dp",
        dp,
        [down_part, ups],
        [lambda peer: peer] * 2,
        finish_total,
        [
            jax.ShapeDtypeStruct((rk, rows), F32),
            jax.ShapeDtypeStruct(ups.shape[1:], F32),
        ],
        6,
    )
    (downs_all,) = exchange(
        "fsdp",
        fsdp,
        [down_mine],
        [None],
        finish_plain,
        [jax.ShapeDtypeStruct((fsdp, rk, rows), F32)],
        7,
    )
    down_grad = downs_all.reshape(2 * RANK, rows).T
    up_flat = up_mine.reshape(-1)
    return (
        down_grad[:, :RANK],
        down_grad[:, RANK:],
        up_flat[: ur * qc].reshape(ur, qc),
        up_flat[ur * qc : ur * (qc + kc)].reshape(ur, kc),
    )


def solution(mesh):
    placed = (
        P("dp", None),
        P("dp"),
        P("dp"),
        P("dp"),
        P("dp", "fsdp"),
        P("dp", "fsdp"),
        P("dp", "fsdp"),
        P("dp", None),
        P("dp", None),
        P(None, "fsdp"),
        P(None, "fsdp"),
        P("dp", "fsdp"),
    )
    return jax.shard_map(
        functools.partial(body, mesh.shape["dp"], mesh.shape["fsdp"]),
        mesh=mesh,
        in_specs=placed,
        out_specs=(P("dp", None), P("dp", None), P("dp", "fsdp"), P("dp", "fsdp")),
        check_vma=False,
    )
```

```python
import functools
import math

import jax
import jax.numpy as jnp
from jax import lax
from jax.experimental import pallas as pl
from jax.experimental.pallas import tpu as pltpu
from jax.sharding import PartitionSpec as P

HEAD_DIM = 128
HEADS = 32
KV_HEADS = 4
SEQ = 128
RANK = 64
ADAPTER_SCALE = 2.0
EPSILON = 1e-06
MESH = pl.DeviceIdType.MESH
F32 = jnp.float32
BF16 = jnp.bfloat16


def dot(a, b, ca, cb):
    return lax.dot_general(a, b, (((ca,), (cb,)), ((), ())), preferred_element_type=F32)


def total(ref, n):
    acc = ref[0]
    for k in range(1, n):
        acc = acc + ref[k]
    return acc


def attend(lengths, query, keys, values, og, qgrad, value_part):
    prompts = query.shape[0] // SEQ
    heads = query.shape[1] // HEAD_DIM
    row = lax.broadcasted_iota(jnp.int32, (SEQ, SEQ), 0)
    col = lax.broadcasted_iota(jnp.int32, (SEQ, SEQ), 1)
    scale = 1.0 / math.sqrt(HEAD_DIM)
    for p in range(prompts):
        length = lengths[p]
        allowed = (col <= row) & (col < length)
        ts = slice(p * SEQ, (p + 1) * SEQ)
        kt = keys[:, ts]
        vt = values[:, ts]
        vsum = None
        for h in range(heads):
            hs = slice(h * HEAD_DIM, (h + 1) * HEAD_DIM)
            scores = dot(query[ts, hs], kt, 1, 0) * scale
            masked = jnp.where(allowed, scores, -1e30)
            peak = jnp.max(masked, axis=1, keepdims=True)
            expo = jnp.where(allowed, jnp.exp(masked - peak), 0.0)
            probs = expo / jnp.sum(expo, axis=1, keepdims=True)
            probs_low = probs.astype(BF16)
            attended = dot(probs_low, vt, 1, 1)
            live32 = jnp.where(row < length, og[ts, hs].astype(F32), 0.0)
            live = live32.astype(BF16)
            terms = jnp.sum(live32 * attended, axis=1, keepdims=True)
            pgrad = dot(live, vt, 1, 0)
            sgrad = (probs * (pgrad - terms)).astype(BF16)
            qgrad[ts, hs] = (dot(sgrad, kt, 1, 1) * scale).astype(BF16)
            part = dot(live, probs_low, 0, 0)
            vsum = part if vsum is None else vsum + part
        value_part[:, :, ts] = vsum.reshape(*value_part.shape[:2], SEQ)


XS = 4
SPLIT = 144


def whole_kernel(
    dp, fsdp, lengths, hidden, class_rows, harm, block, vup, up, og, down_out, up_out,
    base_out, small_out, ablated_out,
    buf, sums, sums_all, diff, diff_all, vup_all, dirs, pieces, got, qgrad, vpart, vpart_all,
    back, back_all, ups, ups_all, down, down_all, mine, mine_all,
    own_sem, send_sem, recv_sem,
    sums_send, sums_recv, diff_send, diff_recv, vup_send, vup_recv, got_send, got_recv,
    vpart_send, vpart_recv, back_send, back_recv, ups_send, ups_recv, down_send, down_recv,
    mine_send, mine_recv,
):
    me = lax.axis_index("dp")
    j = lax.axis_index("fsdp")
    zs = dp // XS
    z, x = me // XS, me % XS
    tok, width = hidden.shape
    rows, cols = buf.shape[1], buf.shape[2]
    share = width // fsdp
    tiles = share // 128
    per_group = fsdp // KV_HEADS
    barrier = pltpu.get_barrier_semaphore()

    def greet(axis, i, n):
        def step(k, carry):
            peer = lax.rem(i + k, n)
            pl.semaphore_signal(barrier, inc=1, device_id={axis: peer}, device_id_type=MESH)
            return carry

        lax.fori_loop(1, n, step, 0)

    greet("dp", me, dp)
    greet("fsdp", j, fsdp)
    own = pltpu.make_async_copy(block, buf.at[me], own_sem)
    own.start()
    cr = class_rows[...]
    part = dot(cr, hidden[:, pl.ds(pl.multiple_of(j * share, share), share)], 1, 0)
    counts = jnp.sum(cr.astype(F32), axis=1, keepdims=True)
    sums[...] = jnp.zeros_like(sums)
    for g in range(2):
        for c in range(tiles):
            r = g * tiles + c
            sums[r : r + 1, :] = part[g : g + 1, c * 128 : (c + 1) * 128]
        sums[8 + g : 9 + g, :] = jnp.broadcast_to(counts[g : g + 1, :], (1, 128))
    pl.semaphore_wait(barrier, dp + fsdp - 2)

    def direct(axis, i, n, src, dst, send, recv):
        def copy(k, slot):
            peer = lax.rem(i + k, n)
            return pltpu.make_async_remote_copy(
                src_ref=src(peer),
                dst_ref=dst.at[i if slot is None else peer],
                send_sem=send.at[peer],
                recv_sem=recv.at[i if slot is None else peer],
                device_id={axis: peer},
                device_id_type=MESH,
            )

        def start(k, carry):
            copy(k, None).start()
            return carry

        def finish(k, carry):
            copy(k, 0).wait()
            return carry

        return (
            lambda: lax.fori_loop(1, n, start, 0),
            lambda: lax.fori_loop(1, n, finish, 0),
        )

    sums_start, sums_wait = direct(
        "dp", me, dp, lambda peer: sums, sums_all, sums_send, sums_recv
    )
    diff_start, diff_wait = direct(
        "fsdp", j, fsdp, lambda peer: diff, diff_all, diff_send, diff_recv
    )
    vup_start, vup_wait = direct(
        "fsdp", j, fsdp, lambda peer: vup.at[peer // per_group], vup_all, vup_send, vup_recv
    )
    sums_start()

    span = (pl.ds(0, SPLIT), pl.ds(SPLIT, rows - SPLIT))
    sent = []

    def place(dz, dx):
        return lax.rem(z + dz + zs, zs) * XS + lax.rem(x + dx, XS)

    def push(half, origin, target, mine=False):
        there = buf.at[origin, span[half]]
        c = pltpu.make_async_remote_copy(
            src_ref=block.at[span[half]] if mine else there,
            dst_ref=there,
            send_sem=send_sem.at[len(sent)],
            recv_sem=recv_sem.at[half, origin],
            device_id={"dp": target},
            device_id_type=MESH,
        )
        c.start()
        sent.append(c)

    def landed(half, origin):
        there = buf.at[origin, span[half]]
        pltpu.make_async_remote_copy(
            src_ref=there,
            dst_ref=there,
            send_sem=send_sem.at[0],
            recv_sem=recv_sem.at[half, origin],
            device_id={"dp": place(1, 0)},
            device_id_type=MESH,
        ).wait_recv()

    reach = ((4, 3), (3, 4))
    above, below = place(1, 0), place(-1, 0)
    for half in (0, 1):
        push(half, me, above, True)
        push(half, me, below, True)
    for half in (0, 1):
        for dx in range(1, XS):
            push(half, me, place(0, dx), True)
    vup_start()
    for dx in range(1, XS):
        origin = place(0, dx)
        landed(0, origin)
        push(0, origin, above)
        push(0, origin, below)

    def forward(k):
        for side, sign, target in ((0, -1, above), (1, 1, below)):
            if k <= reach[1][side]:
                origin = place(sign * k, 0)
                landed(1, origin)
                if k < reach[1][side]:
                    push(1, origin, target)
                for dx in range(1, XS):
                    push(1, origin, place(0, dx))
            if k <= reach[0][side]:
                for dx in range(XS):
                    origin = place(sign * k, dx)
                    landed(0, origin)
                    if k < reach[0][side]:
                        push(0, origin, target)

    def multiply(k):
        for dz in sorted({-k, k} if k < zs // 2 else {k}):
            for dx in range(1, XS):
                landed(1, place(dz, dx))
            first = place(dz, 0) - x

            def step(i, carry):
                origin = first + i
                lanes = pl.ds(pl.multiple_of(origin * cols, cols), cols)
                a = ablated_out[:, lanes]
                base_out[...] += dot(a, buf[origin, 0:cols, :], 1, 0)
                small_out[...] += dot(buf[origin, cols:rows, :], a, 1, 1)
                return carry

            lax.fori_loop(0, XS, step, 0)

    sums_all[me] = sums[...]
    sums_wait()
    t = total(sums_all, dp)
    diff[...] = jnp.zeros_like(diff)
    diff[0:tiles] = t[0:tiles] / t[8:9] - t[tiles : 2 * tiles] / t[9:10]
    forward(1)
    diff_start()
    diff_all[j] = diff[...]
    vup_all[j] = vup[j // per_group]
    base_out[...] = jnp.zeros_like(base_out)
    small_out[...] = jnp.zeros_like(small_out)
    diff_wait()
    d = diff_all[...]
    square = jnp.sum(jnp.sum(jnp.sum(d * d, axis=0), axis=0, keepdims=True), axis=1, keepdims=True)
    scale = lax.rsqrt(square / width + EPSILON) / math.sqrt(width)
    dirs[...] = d * scale

    def tile(c):
        return pl.ds(pl.multiple_of(c * 128, 128), 128)

    def project(b, acc):
        for i in range(tiles):
            c = b * tiles + i
            acc = acc + hidden[:, tile(c)].astype(F32) * dirs[b, i : i + 1, :]
        return acc

    acc = lax.fori_loop(0, fsdp, project, jnp.zeros((tok, 128), F32))
    along = harm[...] * jnp.sum(acc, axis=1, keepdims=True)

    def remove(b, carry):
        for i in range(tiles):
            c = b * tiles + i
            h = hidden[:, tile(c)].astype(F32)
            ablated_out[:, tile(c)] = (h - along * dirs[b, i : i + 1, :]).astype(BF16)
        return carry

    forward(2)
    lax.fori_loop(0, fsdp, remove, 0)
    forward(3)
    own.wait()
    multiply(0)
    multiply(1)
    forward(4)
    multiply(2)
    multiply(3)
    multiply(4)
    dk, toks = vpart.shape[1:]
    rank_rows = back.shape[1]
    kc = KV_HEADS * dk
    g_me = j // per_group
    got_start, got_wait = direct(
        "fsdp", j, fsdp, lambda peer: pieces.at[peer // per_group], got, got_send, got_recv
    )
    vpart_start, vpart_wait = direct(
        "fsdp", j, fsdp, lambda peer: vpart.at[peer], vpart_all, vpart_send, vpart_recv
    )
    back_start, back_wait = direct(
        "fsdp", j, fsdp, lambda peer: back.at[peer], back_all, back_send, back_recv
    )
    ups_start, ups_wait = direct(
        "dp", me, dp, lambda peer: ups.at[peer], ups_all, ups_send, ups_recv
    )
    down_start, down_wait = direct(
        "dp", me, dp, lambda peer: down.at[peer], down_all, down_send, down_recv
    )
    mine_start, mine_wait = direct(
        "fsdp", j, fsdp, lambda peer: mine, mine_all, mine_send, mine_recv
    )
    low_rows = small_out[2 * kc : 2 * kc + rank_rows, :]
    for g in range(KV_HEADS):
        vb = small_out[kc + g * dk : kc + (g + 1) * dk, :]
        top = vb.astype(BF16).astype(F32)
        pieces[g] = jnp.concatenate(
            [small_out[g * dk : (g + 1) * dk, :], top, vb - top, low_rows], axis=0
        ).astype(BF16)
    got_start()
    got[j] = pieces[g_me]
    vup_wait()
    vup_head = vup_all[...].reshape(HEAD_DIM, 128)[:, :RANK].astype(BF16)
    vup_own = vup[...].reshape(kc, 128).astype(BF16)
    got_wait()
    wide = got[...].astype(F32)
    keys = wide[:, :dk].reshape(HEAD_DIM, toks).astype(BF16)
    vbase = (wide[:, dk : 2 * dk] + wide[:, 2 * dk : 3 * dk]).reshape(HEAD_DIM, toks)
    low = wide[:, 3 * dk :].reshape(2 * RANK, toks).astype(BF16)
    values = (vbase + ADAPTER_SCALE * dot(vup_head, low[RANK:], 1, 0)).astype(BF16)
    query = (base_out[...] + ADAPTER_SCALE * dot(low[:RANK], up[...], 0, 0)).astype(BF16)
    attend(lengths, query, keys, values, og, qgrad, vpart)
    vpart_start()
    vpart_all[j] = vpart[j]
    qg = qgrad[...]
    qback = ADAPTER_SCALE * dot(up[...], qg, 1, 1)
    back[0 : fsdp // 2] = qback.reshape(fsdp // 2, rank_rows, toks)
    qup = ADAPTER_SCALE * dot(low[:RANK], qg, 1, 0)
    ur = RANK // dp
    ups[...] = jnp.zeros_like(ups)
    for p in range(dp):
        ups[p, 0:ur, :] = qup[p * ur : (p + 1) * ur, :]
    vpart_wait()
    va = vpart_all[...]
    heads_sum = []
    for g in range(KV_HEADS):
        acc = va[per_group * g]
        for k in range(1, per_group):
            acc = acc + va[per_group * g + k]
        heads_sum.append(acc)
    vgrad = jnp.concatenate(heads_sum, axis=0).astype(BF16)
    vback = ADAPTER_SCALE * dot(vup_own, vgrad, 0, 0)[:RANK]
    back[fsdp // 2 :] = vback.reshape(fsdp // 2, rank_rows, toks)
    back_start()
    back_all[j] = back[j]
    vup_grad = ADAPTER_SCALE * dot(low[RANK:], vgrad, 1, 1)
    for p in range(dp):
        ups[p, ur : 2 * ur, 0:kc] = vup_grad[p * ur : (p + 1) * ur, :]
    ups_start()
    ups_all[me] = ups[me]
    back_wait()
    both = total(back_all, fsdp).astype(BF16)

    def chunk(p, carry):
        lanes = pl.ds(pl.multiple_of(p * cols, cols), cols)
        down[p] = dot(both, ablated_out[:, lanes], 1, 0)
        return carry

    lax.fori_loop(0, dp, chunk, 0)
    down_start()
    down_all[me] = down[me]
    ups_wait()
    up_out[...] = total(ups_all, dp)
    down_wait()
    mine[...] = total(down_all, dp)
    mine_start()
    mine_all[j] = mine[...]
    mine_wait()
    down_out[...] = mine_all[...].reshape(2 * RANK, cols)
    for c in sent:
        c.wait_send()


def step_kernel(dp, fsdp, lengths, hidden, class_rows, harm, block, vup, up, og):
    tok, width = hidden.shape
    rows, cols = block.shape
    dk, rk = vup.shape[1], 2 * RANK // fsdp
    vmem = pl.BlockSpec(memory_space=pltpu.VMEM)
    dma = pltpu.SemaphoreType.DMA
    f32 = lambda *shape: pltpu.VMEM(shape, F32)
    bf16 = lambda *shape: pltpu.VMEM(shape, BF16)
    return pl.pallas_call(
        functools.partial(whole_kernel, dp, fsdp),
        out_shape=(
            jax.ShapeDtypeStruct((2 * RANK, cols), F32),
            jax.ShapeDtypeStruct((8, cols), F32),
        ),
        in_specs=[pl.BlockSpec(memory_space=pltpu.SMEM)] + [vmem] * 7,
        out_specs=[vmem] * 2,
        scratch_shapes=[
            f32(tok, cols),
            f32(rows - cols, tok),
            bf16(tok, width),
            bf16(dp, rows, cols),
            f32(16, 128),
            f32(dp, 16, 128),
            f32(8, 128),
            f32(fsdp, 8, 128),
            f32(fsdp, dk, 128),
            f32(fsdp, 8, 128),
            bf16(KV_HEADS, 3 * dk + rk, tok),
            bf16(fsdp, 3 * dk + rk, tok),
            bf16(tok, cols),
            f32(fsdp, dk, tok),
            f32(fsdp, dk, tok),
            f32(fsdp, rk, tok),
            f32(fsdp, rk, tok),
            f32(dp, 8, cols),
            f32(dp, 8, cols),
            f32(dp, rk, cols),
            f32(dp, rk, cols),
            f32(rk, cols),
            f32(fsdp, rk, cols),
            dma,
            dma((72,)),
            dma((2, dp)),
            *[dma((n,)) for n in (dp, fsdp, fsdp, fsdp, fsdp, fsdp, dp, dp, fsdp) for _ in (0, 1)],
        ],
        compiler_params=pltpu.CompilerParams(
            collective_id=1, has_side_effects=True, vmem_limit_bytes=48 * 1024 * 1024
        ),
    )(lengths, hidden, class_rows, harm, block, vup, up, og)


def body(
    dp,
    fsdp,
    hidden_states,
    lengths,
    labels,
    token_mask,
    q_weight,
    k_weight,
    v_weight,
    q_down,
    v_down,
    query_up_weight,
    value_up_weight,
    out_grad,
):
    tok, width = hidden_states.shape
    j = lax.axis_index("fsdp")
    rows = q_weight.shape[0]
    qc, kc = q_weight.shape[1], k_weight.shape[1]
    dk = kc // KV_HEADS
    rk = 2 * RANK // fsdp
    downs = jnp.concatenate([q_down, v_down], axis=1)
    my_down = lax.dynamic_slice(downs, (0, j * rk), (rows, rk))

    def by_head(w):
        return w.T.reshape(dk, KV_HEADS, rows).transpose(1, 0, 2).reshape(kc, rows)

    lower = jnp.concatenate([by_head(k_weight), by_head(v_weight), my_down.T], axis=0)
    lower = jnp.pad(lower, ((0, -lower.shape[0] % 16), (0, 0)))
    block = jnp.concatenate([q_weight, lower], axis=0)

    harmful = jnp.repeat(labels, SEQ).astype(F32)
    chosen = token_mask.astype(F32)
    class_rows = jnp.stack([chosen * harmful, chosen * (1.0 - harmful)])
    class_rows = jnp.pad(class_rows, ((0, 14), (0, 0))).astype(BF16)
    vup = value_up_weight.reshape(RANK, dk, KV_HEADS).transpose(2, 1, 0)
    vup_piece = jnp.pad(vup.astype(F32), ((0, 0), (0, 0), (0, 128 - RANK)))
    down, ups = step_kernel(
        dp,
        fsdp,
        lengths,
        hidden_states,
        class_rows,
        harmful[:, None],
        block,
        vup_piece,
        query_up_weight,
        out_grad,
    )
    ur = RANK // dp
    value_up = ups[ur : 2 * ur, :kc].reshape(ur, KV_HEADS, dk).transpose(0, 2, 1)
    return down[:RANK].T, down[RANK:].T, ups[:ur], value_up.reshape(ur, kc)


def solution(mesh):
    placed = (
        P("dp", None),
        P("dp"),
        P("dp"),
        P("dp"),
        P("dp", "fsdp"),
        P("dp", "fsdp"),
        P("dp", "fsdp"),
        P("dp", None),
        P("dp", None),
        P(None, "fsdp"),
        P(None, "fsdp"),
        P("dp", "fsdp"),
    )
    return jax.shard_map(
        functools.partial(body, mesh.shape["dp"], mesh.shape["fsdp"]),
        mesh=mesh,
        in_specs=placed,
        out_specs=(P("dp", None), P("dp", None), P("dp", "fsdp"), P("dp", "fsdp")),
        check_vma=False,
    )
```

```python
import functools
import math

import jax
import jax.numpy as jnp
from jax import lax
from jax.experimental import pallas as pl
from jax.experimental.pallas import tpu as pltpu
from jax.sharding import PartitionSpec as P

HEAD_DIM = 128
HEADS = 32
KV_HEADS = 4
SEQ = 128
RANK = 64
ADAPTER_SCALE = 2.0
EPSILON = 1e-06
MESH = pl.DeviceIdType.MESH
F32 = jnp.float32
BF16 = jnp.bfloat16


def dot(a, b, ca, cb):
    return lax.dot_general(a, b, (((ca,), (cb,)), ((), ())), preferred_element_type=F32)


def total(ref, n):
    acc = ref[0]
    for k in range(1, n):
        acc = acc + ref[k]
    return acc


def attend(lengths, query, keys, values, og, qgrad, value_part):
    prompts = query.shape[0] // SEQ
    heads = query.shape[1] // HEAD_DIM
    row = lax.broadcasted_iota(jnp.int32, (SEQ, SEQ), 0)
    col = lax.broadcasted_iota(jnp.int32, (SEQ, SEQ), 1)
    scale = 1.0 / math.sqrt(HEAD_DIM)
    for p in range(prompts):
        length = lengths[p]
        allowed = (col <= row) & (col < length)
        ts = slice(p * SEQ, (p + 1) * SEQ)
        kt = keys[:, ts]
        vt = values[:, ts]
        vsum = None
        for h in range(heads):
            hs = slice(h * HEAD_DIM, (h + 1) * HEAD_DIM)
            scores = dot(query[ts, hs], kt, 1, 0) * scale
            masked = jnp.where(allowed, scores, -1e30)
            peak = jnp.max(masked, axis=1, keepdims=True)
            expo = jnp.where(allowed, jnp.exp(masked - peak), 0.0)
            probs = expo / jnp.sum(expo, axis=1, keepdims=True)
            probs_low = probs.astype(BF16)
            attended = dot(probs_low, vt, 1, 1)
            live32 = jnp.where(row < length, og[ts, hs].astype(F32), 0.0)
            live = live32.astype(BF16)
            terms = jnp.sum(live32 * attended, axis=1, keepdims=True)
            pgrad = dot(live, vt, 1, 0)
            sgrad = (probs * (pgrad - terms)).astype(BF16)
            qgrad[ts, hs] = (dot(sgrad, kt, 1, 1) * scale).astype(BF16)
            part = dot(live, probs_low, 0, 0)
            vsum = part if vsum is None else vsum + part
        value_part[:, :, ts] = vsum.reshape(*value_part.shape[:2], SEQ)


XS = 4
SPLIT = 144


def whole_kernel(
    dp, fsdp, lengths, labels, token_mask, hidden_in, block, vup, up_in, og_in, down_out, up_out,
    base_out, small_out, ablated_out,
    buf, sums, sums_all, diff, diff_all, vup_all, dirs, pieces, got, qgrad, vpart, vpart_all,
    back, back_all, ups, ups_all, down, down_all, mine, mine_all,
    hidden, up, og, load_sem, own_sem, send_sem, recv_sem,
    sums_send, sums_recv, diff_send, diff_recv, vup_send, vup_recv, got_send, got_recv,
    vpart_send, vpart_recv, back_send, back_recv, ups_send, ups_recv, down_send, down_recv,
    mine_send, mine_recv,
):
    me = lax.axis_index("dp")
    j = lax.axis_index("fsdp")
    zs = dp // XS
    z, x = me // XS, me % XS
    tok, width = hidden.shape
    rows, cols = buf.shape[1], buf.shape[2]
    share = width // fsdp
    tiles = share // 128
    per_group = fsdp // KV_HEADS
    barrier = pltpu.get_barrier_semaphore()
    loads = [
        pltpu.make_async_copy(src, dst, load_sem.at[i])
        for i, (src, dst) in enumerate(((hidden_in, hidden), (up_in, up), (og_in, og)))
    ]
    for load in loads:
        load.start()

    def greet(axis, i, n):
        def step(k, carry):
            peer = lax.rem(i + k, n)
            pl.semaphore_signal(barrier, inc=1, device_id={axis: peer}, device_id_type=MESH)
            return carry

        lax.fori_loop(1, n, step, 0)

    greet("dp", me, dp)
    greet("fsdp", j, fsdp)
    own = pltpu.make_async_copy(block, buf.at[me], own_sem)
    own.start()

    def label_of(index):
        value = jnp.zeros(index.shape, F32)
        for p in range(tok // SEQ):
            inside = (index >= p * SEQ) & (index < (p + 1) * SEQ)
            value = jnp.where(inside, labels[p].astype(F32), value)
        return value

    harm = label_of(lax.broadcasted_iota(jnp.int32, (tok, 1), 0))
    harm_row = label_of(lax.broadcasted_iota(jnp.int32, (16, tok), 1))
    class_id = lax.broadcasted_iota(jnp.int32, (16, tok), 0)
    chosen = jnp.broadcast_to(token_mask[...].astype(F32), (16, tok))
    cr = jnp.where(
        class_id == 0,
        chosen * harm_row,
        jnp.where(class_id == 1, chosen * (1.0 - harm_row), 0.0),
    ).astype(BF16)
    loads[0].wait()
    part = dot(cr, hidden[:, pl.ds(pl.multiple_of(j * share, share), share)], 1, 0)
    counts = jnp.sum(cr.astype(F32), axis=1, keepdims=True)
    sums[...] = jnp.zeros_like(sums)
    for g in range(2):
        for c in range(tiles):
            r = g * tiles + c
            sums[r : r + 1, :] = part[g : g + 1, c * 128 : (c + 1) * 128]
        sums[8 + g : 9 + g, :] = jnp.broadcast_to(counts[g : g + 1, :], (1, 128))
    pl.semaphore_wait(barrier, dp + fsdp - 2)

    def direct(axis, i, n, src, dst, send, recv):
        def copy(k, slot):
            peer = lax.rem(i + k, n)
            return pltpu.make_async_remote_copy(
                src_ref=src(peer),
                dst_ref=dst.at[i if slot is None else peer],
                send_sem=send.at[peer],
                recv_sem=recv.at[i if slot is None else peer],
                device_id={axis: peer},
                device_id_type=MESH,
            )

        def start(k, carry):
            copy(k, None).start()
            return carry

        def finish(k, carry):
            copy(k, 0).wait()
            return carry

        return (
            lambda: lax.fori_loop(1, n, start, 0),
            lambda: lax.fori_loop(1, n, finish, 0),
        )

    sums_start, sums_wait = direct(
        "dp", me, dp, lambda peer: sums, sums_all, sums_send, sums_recv
    )
    diff_start, diff_wait = direct(
        "fsdp", j, fsdp, lambda peer: diff, diff_all, diff_send, diff_recv
    )
    vup_start, vup_wait = direct(
        "fsdp", j, fsdp, lambda peer: vup.at[peer // per_group], vup_all, vup_send, vup_recv
    )
    sums_start()

    span = (pl.ds(0, SPLIT), pl.ds(SPLIT, rows - SPLIT))
    sent = []

    def place(dz, dx):
        return lax.rem(z + dz + zs, zs) * XS + lax.rem(x + dx, XS)

    def push(half, origin, target, mine=False):
        there = buf.at[origin, span[half]]
        c = pltpu.make_async_remote_copy(
            src_ref=block.at[span[half]] if mine else there,
            dst_ref=there,
            send_sem=send_sem.at[len(sent)],
            recv_sem=recv_sem.at[half, origin],
            device_id={"dp": target},
            device_id_type=MESH,
        )
        c.start()
        sent.append(c)

    def landed(half, origin):
        there = buf.at[origin, span[half]]
        pltpu.make_async_remote_copy(
            src_ref=there,
            dst_ref=there,
            send_sem=send_sem.at[0],
            recv_sem=recv_sem.at[half, origin],
            device_id={"dp": place(1, 0)},
            device_id_type=MESH,
        ).wait_recv()

    reach = ((4, 3), (3, 4))
    above, below = place(1, 0), place(-1, 0)
    for half in (0, 1):
        push(half, me, above, True)
        push(half, me, below, True)
    for half in (0, 1):
        for dx in range(1, XS):
            push(half, me, place(0, dx), True)
    vup_start()
    for dx in range(1, XS):
        origin = place(0, dx)
        landed(0, origin)
        push(0, origin, above)
        push(0, origin, below)

    def forward(k):
        for side, sign, target in ((0, -1, above), (1, 1, below)):
            if k <= reach[1][side]:
                origin = place(sign * k, 0)
                landed(1, origin)
                if k < reach[1][side]:
                    push(1, origin, target)
                for dx in range(1, XS):
                    push(1, origin, place(0, dx))
            if k <= reach[0][side]:
                for dx in range(XS):
                    origin = place(sign * k, dx)
                    landed(0, origin)
                    if k < reach[0][side]:
                        push(0, origin, target)

    def multiply(k):
        for dz in sorted({-k, k} if k < zs // 2 else {k}):
            for dx in range(1, XS):
                landed(1, place(dz, dx))
            first = place(dz, 0) - x
            blocks = pl.ds(first, XS)
            lanes = pl.ds(pl.multiple_of(first * cols, XS * cols), XS * cols)
            a = ablated_out[:, lanes]
            base_out[...] += dot(a, buf[blocks, 0:cols, :].reshape(XS * cols, cols), 1, 0)
            acc = small_out[...]
            for i in range(XS):
                acc += dot(buf[first + i, cols:rows, :], a[:, i * cols : (i + 1) * cols], 1, 1)
            small_out[...] = acc

    sums_all[me] = sums[...]
    sums_wait()
    t = total(sums_all, dp)
    diff[...] = jnp.zeros_like(diff)
    diff[0:tiles] = t[0:tiles] / t[8:9] - t[tiles : 2 * tiles] / t[9:10]
    forward(1)
    diff_start()
    diff_all[j] = diff[...]
    vup_all[j] = vup[j // per_group]
    base_out[...] = jnp.zeros_like(base_out)
    small_out[...] = jnp.zeros_like(small_out)
    diff_wait()
    d = diff_all[...]
    square = jnp.sum(jnp.sum(jnp.sum(d * d, axis=0), axis=0, keepdims=True), axis=1, keepdims=True)
    scale = lax.rsqrt(square / width + EPSILON) / math.sqrt(width)
    dirs[...] = d * scale

    def tile(c):
        return pl.ds(pl.multiple_of(c * 128, 128), 128)

    def project(b, acc):
        for i in range(tiles):
            c = b * tiles + i
            acc = acc + hidden[:, tile(c)].astype(F32) * dirs[b, i : i + 1, :]
        return acc

    acc = lax.fori_loop(0, fsdp, project, jnp.zeros((tok, 128), F32))
    along = harm * jnp.sum(acc, axis=1, keepdims=True)

    def remove(b, carry):
        for i in range(tiles):
            c = b * tiles + i
            h = hidden[:, tile(c)].astype(F32)
            ablated_out[:, tile(c)] = (h - along * dirs[b, i : i + 1, :]).astype(BF16)
        return carry

    forward(2)
    lax.fori_loop(0, fsdp, remove, 0)
    forward(3)
    own.wait()
    multiply(0)
    multiply(1)
    forward(4)
    multiply(2)
    multiply(3)
    multiply(4)
    dk, toks = vpart.shape[1:]
    rank_rows = back.shape[1]
    kc = KV_HEADS * dk
    g_me = j // per_group
    got_start, got_wait = direct(
        "fsdp", j, fsdp, lambda peer: pieces.at[peer // per_group], got, got_send, got_recv
    )
    vpart_start, vpart_wait = direct(
        "fsdp", j, fsdp, lambda peer: vpart.at[peer], vpart_all, vpart_send, vpart_recv
    )
    back_start, back_wait = direct(
        "fsdp", j, fsdp, lambda peer: back.at[peer], back_all, back_send, back_recv
    )
    ups_start, ups_wait = direct(
        "dp", me, dp, lambda peer: ups.at[peer], ups_all, ups_send, ups_recv
    )
    down_start, down_wait = direct(
        "dp", me, dp, lambda peer: down.at[peer], down_all, down_send, down_recv
    )
    mine_start, mine_wait = direct(
        "fsdp", j, fsdp, lambda peer: mine, mine_all, mine_send, mine_recv
    )
    low_rows = small_out[2 * kc : 2 * kc + rank_rows, :]
    for g in range(KV_HEADS):
        vb = small_out[kc + g * dk : kc + (g + 1) * dk, :]
        top = vb.astype(BF16).astype(F32)
        pieces[g] = jnp.concatenate(
            [small_out[g * dk : (g + 1) * dk, :], top, vb - top, low_rows], axis=0
        ).astype(BF16)
    got_start()
    got[j] = pieces[g_me]
    vup_wait()
    vup_head = vup_all[...].reshape(HEAD_DIM, 128)[:, :RANK].astype(BF16)
    vup_own = vup[...].reshape(kc, 128).astype(BF16)
    got_wait()
    loads[1].wait()
    loads[2].wait()
    wide = got[...].astype(F32)
    keys = wide[:, :dk].reshape(HEAD_DIM, toks).astype(BF16)
    vbase = (wide[:, dk : 2 * dk] + wide[:, 2 * dk : 3 * dk]).reshape(HEAD_DIM, toks)
    low = wide[:, 3 * dk :].reshape(2 * RANK, toks).astype(BF16)
    values = (vbase + ADAPTER_SCALE * dot(vup_head, low[RANK:], 1, 0)).astype(BF16)
    query = (base_out[...] + ADAPTER_SCALE * dot(low[:RANK], up[...], 0, 0)).astype(BF16)
    attend(lengths, query, keys, values, og, qgrad, vpart)
    vpart_start()
    vpart_all[j] = vpart[j]
    qg = qgrad[...]
    qback = ADAPTER_SCALE * dot(up[...], qg, 1, 1)
    back[0 : fsdp // 2] = qback.reshape(fsdp // 2, rank_rows, toks)
    qup = ADAPTER_SCALE * dot(low[:RANK], qg, 1, 0)
    ur = RANK // dp
    ups[...] = jnp.zeros_like(ups)
    for p in range(dp):
        ups[p, 0:ur, :] = qup[p * ur : (p + 1) * ur, :]
    vpart_wait()
    va = vpart_all[...]
    heads_sum = []
    for g in range(KV_HEADS):
        acc = va[per_group * g]
        for k in range(1, per_group):
            acc = acc + va[per_group * g + k]
        heads_sum.append(acc)
    vgrad = jnp.concatenate(heads_sum, axis=0).astype(BF16)
    vback = ADAPTER_SCALE * dot(vup_own, vgrad, 0, 0)[:RANK]
    back[fsdp // 2 :] = vback.reshape(fsdp // 2, rank_rows, toks)
    back_start()
    back_all[j] = back[j]
    vup_grad = ADAPTER_SCALE * dot(low[RANK:], vgrad, 1, 1)
    for p in range(dp):
        ups[p, ur : 2 * ur, 0:kc] = vup_grad[p * ur : (p + 1) * ur, :]
    ups_start()
    ups_all[me] = ups[me]
    back_wait()
    both = total(back_all, fsdp).astype(BF16)

    def chunk(p, carry):
        lanes = pl.ds(pl.multiple_of(p * cols, cols), cols)
        down[p] = dot(both, ablated_out[:, lanes], 1, 0)
        return carry

    lax.fori_loop(0, dp, chunk, 0)
    down_start()
    down_all[me] = down[me]
    ups_wait()
    up_out[...] = total(ups_all, dp)
    down_wait()
    mine[...] = total(down_all, dp)
    mine_start()
    mine_all[j] = mine[...]
    mine_wait()
    down_out[...] = mine_all[...].reshape(2 * RANK, cols)
    for c in sent:
        c.wait_send()


def step_kernel(dp, fsdp, lengths, labels, token_mask, hidden, block, vup, up, og):
    tok, width = hidden.shape
    rows, cols = block.shape
    dk, rk = vup.shape[1], 2 * RANK // fsdp
    vmem = pl.BlockSpec(memory_space=pltpu.VMEM)
    smem = pl.BlockSpec(memory_space=pltpu.SMEM)
    hbm = pl.BlockSpec(memory_space=pltpu.HBM)
    dma = pltpu.SemaphoreType.DMA
    f32 = lambda *shape: pltpu.VMEM(shape, F32)
    bf16 = lambda *shape: pltpu.VMEM(shape, BF16)
    return pl.pallas_call(
        functools.partial(whole_kernel, dp, fsdp),
        out_shape=(
            jax.ShapeDtypeStruct((2 * RANK, cols), F32),
            jax.ShapeDtypeStruct((8, cols), F32),
        ),
        in_specs=[smem, smem, vmem, hbm, vmem, vmem, hbm, hbm],
        out_specs=[vmem] * 2,
        scratch_shapes=[
            f32(tok, cols),
            f32(rows - cols, tok),
            bf16(tok, width),
            bf16(dp, rows, cols),
            f32(16, 128),
            f32(dp, 16, 128),
            f32(8, 128),
            f32(fsdp, 8, 128),
            f32(fsdp, dk, 128),
            f32(fsdp, 8, 128),
            bf16(KV_HEADS, 3 * dk + rk, tok),
            bf16(fsdp, 3 * dk + rk, tok),
            bf16(tok, cols),
            f32(fsdp, dk, tok),
            f32(fsdp, dk, tok),
            f32(fsdp, rk, tok),
            f32(fsdp, rk, tok),
            f32(dp, 8, cols),
            f32(dp, 8, cols),
            f32(dp, rk, cols),
            f32(dp, rk, cols),
            f32(rk, cols),
            f32(fsdp, rk, cols),
            bf16(tok, width),
            bf16(*up.shape),
            bf16(*og.shape),
            dma((3,)),
            dma,
            dma((72,)),
            dma((2, dp)),
            *[dma((n,)) for n in (dp, fsdp, fsdp, fsdp, fsdp, fsdp, dp, dp, fsdp) for _ in (0, 1)],
        ],
        compiler_params=pltpu.CompilerParams(
            collective_id=1, has_side_effects=True, vmem_limit_bytes=67_043_328
        ),
    )(lengths, labels, token_mask, hidden, block, vup, up, og)


def body(
    dp,
    fsdp,
    hidden_states,
    lengths,
    labels,
    token_mask,
    q_weight,
    k_weight,
    v_weight,
    q_down,
    v_down,
    query_up_weight,
    value_up_weight,
    out_grad,
):
    tok, width = hidden_states.shape
    j = lax.axis_index("fsdp")
    rows = q_weight.shape[0]
    qc, kc = q_weight.shape[1], k_weight.shape[1]
    dk = kc // KV_HEADS
    rk = 2 * RANK // fsdp
    downs = jnp.concatenate([q_down, v_down], axis=1)
    my_down = lax.dynamic_slice(downs, (0, j * rk), (rows, rk))

    def by_head(w):
        return w.T.reshape(dk, KV_HEADS, rows).transpose(1, 0, 2).reshape(kc, rows)

    lower = jnp.concatenate([by_head(k_weight), by_head(v_weight), my_down.T], axis=0)
    lower = jnp.pad(lower, ((0, -lower.shape[0] % 16), (0, 0)))
    block = jnp.concatenate([q_weight, lower], axis=0)

    vup = value_up_weight.reshape(RANK, dk, KV_HEADS).transpose(2, 1, 0)
    vup_piece = jnp.pad(vup.astype(F32), ((0, 0), (0, 0), (0, 128 - RANK)))
    down, ups = step_kernel(
        dp,
        fsdp,
        lengths,
        labels,
        token_mask[None, :],
        hidden_states,
        block,
        vup_piece,
        query_up_weight,
        out_grad,
    )
    ur = RANK // dp
    value_up = ups[ur : 2 * ur, :kc].reshape(ur, KV_HEADS, dk).transpose(0, 2, 1)
    return down[:RANK].T, down[RANK:].T, ups[:ur], value_up.reshape(ur, kc)


def solution(mesh):
    placed = (
        P("dp", None),
        P("dp"),
        P("dp"),
        P("dp"),
        P("dp", "fsdp"),
        P("dp", "fsdp"),
        P("dp", "fsdp"),
        P("dp", None),
        P("dp", None),
        P(None, "fsdp"),
        P(None, "fsdp"),
        P("dp", "fsdp"),
    )
    return jax.shard_map(
        functools.partial(body, mesh.shape["dp"], mesh.shape["fsdp"]),
        mesh=mesh,
        in_specs=placed,
        out_specs=(P("dp", None), P("dp", None), P("dp", "fsdp"), P("dp", "fsdp")),
        check_vma=False,
    )
```

```python
import functools
import math

import jax
import jax.numpy as jnp
from jax import lax
from jax.experimental import pallas as pl
from jax.experimental.pallas import tpu as pltpu
from jax.sharding import PartitionSpec as P

HEAD_DIM = 128
HEADS = 32
KV_HEADS = 4
SEQ = 128
RANK = 64
ADAPTER_SCALE = 2.0
EPSILON = 1e-06
MESH = pl.DeviceIdType.MESH
F32 = jnp.float32
BF16 = jnp.bfloat16


def dot(a, b, ca, cb):
    return lax.dot_general(a, b, (((ca,), (cb,)), ((), ())), preferred_element_type=F32)


def total(ref, n):
    acc = ref[0]
    for k in range(1, n):
        acc = acc + ref[k]
    return acc


def attend(lengths, query, keys, values, og, qgrad, value_part):
    prompts = query.shape[0] // SEQ
    heads = query.shape[1] // HEAD_DIM
    row = lax.broadcasted_iota(jnp.int32, (SEQ, SEQ), 0)
    col = lax.broadcasted_iota(jnp.int32, (SEQ, SEQ), 1)
    scale = 1.0 / math.sqrt(HEAD_DIM)
    for p in range(prompts):
        length = lengths[p]
        allowed = (col <= row) & (col < length)
        ts = slice(p * SEQ, (p + 1) * SEQ)
        kt = keys[:, ts]
        vt = values[:, ts]
        vsum = None
        for h in range(heads):
            hs = slice(h * HEAD_DIM, (h + 1) * HEAD_DIM)
            scores = dot(query[ts, hs], kt, 1, 0) * scale
            masked = jnp.where(allowed, scores, -1e30)
            peak = jnp.max(masked, axis=1, keepdims=True)
            expo = jnp.where(allowed, jnp.exp(masked - peak), 0.0)
            probs = expo / jnp.sum(expo, axis=1, keepdims=True)
            probs_low = probs.astype(BF16)
            attended = dot(probs_low, vt, 1, 1)
            live32 = jnp.where(row < length, og[ts, hs].astype(F32), 0.0)
            live = live32.astype(BF16)
            terms = jnp.sum(live32 * attended, axis=1, keepdims=True)
            pgrad = dot(live, vt, 1, 0)
            sgrad = (probs * (pgrad - terms)).astype(BF16)
            qgrad[ts, hs] = (dot(sgrad, kt, 1, 1) * scale).astype(BF16)
            part = dot(live, probs_low, 0, 0)
            vsum = part if vsum is None else vsum + part
        value_part[:, :, ts] = vsum.reshape(*value_part.shape[:2], SEQ)


XS = 4
SPLIT = 144


def whole_kernel(
    dp, fsdp, lengths, labels, token_mask, hidden_in, block, vup, up_in, og_in, down_out, up_out,
    base_out, small_out, ablated_out,
    buf, sums, sums_all, diff, diff_all, vup_all, dirs, pieces, got, qgrad, vpart, vpart_all,
    back, back_all, ups, ups_all, down, down_all, mine, mine_all,
    hidden, up, og, load_sem, own_sem, send_sem, recv_sem,
    sums_send, sums_recv, diff_send, diff_recv, vup_send, vup_recv, got_send, got_recv,
    vpart_send, vpart_recv, back_send, back_recv, ups_send, ups_recv, down_send, down_recv,
    mine_send, mine_recv,
):
    me = lax.axis_index("dp")
    j = lax.axis_index("fsdp")
    zs = dp // XS
    z, x = me // XS, me % XS
    tok, width = hidden.shape
    rows, cols = buf.shape[1], buf.shape[2]
    share = width // fsdp
    tiles = share // 128
    per_group = fsdp // KV_HEADS
    barrier = pltpu.get_barrier_semaphore()
    loads = [
        pltpu.make_async_copy(src, dst, load_sem.at[i])
        for i, (src, dst) in enumerate(((hidden_in, hidden), (up_in, up), (og_in, og)))
    ]
    for load in loads:
        load.start()

    def greet(axis, i, n):
        def step(k, carry):
            peer = lax.rem(i + k, n)
            pl.semaphore_signal(barrier, inc=1, device_id={axis: peer}, device_id_type=MESH)
            return carry

        lax.fori_loop(1, n, step, 0)

    greet("dp", me, dp)
    greet("fsdp", j, fsdp)
    own = pltpu.make_async_copy(block, buf.at[me], own_sem)
    own.start()

    def label_of(index):
        value = jnp.zeros(index.shape, F32)
        for p in range(tok // SEQ):
            inside = (index >= p * SEQ) & (index < (p + 1) * SEQ)
            value = jnp.where(inside, labels[p].astype(F32), value)
        return value

    harm = label_of(lax.broadcasted_iota(jnp.int32, (tok, 1), 0))
    harm_row = label_of(lax.broadcasted_iota(jnp.int32, (16, tok), 1))
    class_id = lax.broadcasted_iota(jnp.int32, (16, tok), 0)
    chosen = jnp.broadcast_to(token_mask[...].astype(F32), (16, tok))
    cr = jnp.where(
        class_id == 0,
        chosen * harm_row,
        jnp.where(class_id == 1, chosen * (1.0 - harm_row), 0.0),
    ).astype(BF16)
    loads[0].wait()
    part = dot(cr, hidden[:, pl.ds(pl.multiple_of(j * share, share), share)], 1, 0)
    counts = jnp.sum(cr.astype(F32), axis=1, keepdims=True)
    sums[...] = jnp.zeros_like(sums)
    for g in range(2):
        for c in range(tiles):
            r = g * tiles + c
            sums[r : r + 1, :] = part[g : g + 1, c * 128 : (c + 1) * 128]
        sums[8 + g : 9 + g, :] = jnp.broadcast_to(counts[g : g + 1, :], (1, 128))
    pl.semaphore_wait(barrier, dp + fsdp - 2)

    def direct(axis, i, n, src, dst, send, recv):
        def copy(k, slot):
            peer = lax.rem(i + k, n)
            return pltpu.make_async_remote_copy(
                src_ref=src(peer),
                dst_ref=dst.at[i if slot is None else peer],
                send_sem=send.at[peer],
                recv_sem=recv.at[i if slot is None else peer],
                device_id={axis: peer},
                device_id_type=MESH,
            )

        def start(k, carry):
            copy(k, None).start()
            return carry

        def finish(k, carry):
            copy(k, 0).wait()
            return carry

        return (
            lambda: lax.fori_loop(1, n, start, 0),
            lambda: lax.fori_loop(1, n, finish, 0),
        )

    sums_start, sums_wait = direct(
        "dp", me, dp, lambda peer: sums, sums_all, sums_send, sums_recv
    )
    diff_start, diff_wait = direct(
        "fsdp", j, fsdp, lambda peer: diff, diff_all, diff_send, diff_recv
    )
    vup_start, vup_wait = direct(
        "fsdp", j, fsdp, lambda peer: vup.at[peer // per_group], vup_all, vup_send, vup_recv
    )
    sums_start()

    span = (pl.ds(0, SPLIT), pl.ds(SPLIT, rows - SPLIT))
    sent = []

    def place(dz, dx):
        return lax.rem(z + dz + zs, zs) * XS + lax.rem(x + dx, XS)

    def push(half, origin, target, mine=False):
        there = buf.at[origin, span[half]]
        c = pltpu.make_async_remote_copy(
            src_ref=block.at[span[half]] if mine else there,
            dst_ref=there,
            send_sem=send_sem.at[len(sent)],
            recv_sem=recv_sem.at[half, origin],
            device_id={"dp": target},
            device_id_type=MESH,
        )
        c.start()
        sent.append(c)

    def landed(half, origin):
        there = buf.at[origin, span[half]]
        pltpu.make_async_remote_copy(
            src_ref=there,
            dst_ref=there,
            send_sem=send_sem.at[0],
            recv_sem=recv_sem.at[half, origin],
            device_id={"dp": place(1, 0)},
            device_id_type=MESH,
        ).wait_recv()

    reach = ((4, 3), (3, 4))
    above, below = place(1, 0), place(-1, 0)
    for half in (0, 1):
        push(half, me, above, True)
        push(half, me, below, True)
    for half in (0, 1):
        for dx in range(1, XS):
            push(half, me, place(0, dx), True)
    vup_start()
    for dx in range(1, XS):
        origin = place(0, dx)
        landed(0, origin)
        push(0, origin, above)
        push(0, origin, below)

    def forward(k):
        for side, sign, target in ((0, -1, above), (1, 1, below)):
            if k <= reach[1][side]:
                origin = place(sign * k, 0)
                landed(1, origin)
                if k < reach[1][side]:
                    push(1, origin, target)
                for dx in range(1, XS):
                    push(1, origin, place(0, dx))
        for dx in range(XS):
            for side, sign, target in ((0, -1, above), (1, 1, below)):
                if k <= reach[0][side]:
                    origin = place(sign * k, dx)
                    landed(0, origin)
                    if k < reach[0][side]:
                        push(0, origin, target)

    def multiply(k):
        for dz in sorted({-k, k} if k < zs // 2 else {k}):
            for dx in range(1, XS):
                landed(1, place(dz, dx))
            first = place(dz, 0) - x
            blocks = pl.ds(first, XS)
            lanes = pl.ds(pl.multiple_of(first * cols, XS * cols), XS * cols)
            a = ablated_out[:, lanes]
            base_out[...] += dot(a, buf[blocks, 0:cols, :].reshape(XS * cols, cols), 1, 0)
            acc = small_out[...]
            for i in range(XS):
                acc += dot(buf[first + i, cols:rows, :], a[:, i * cols : (i + 1) * cols], 1, 1)
            small_out[...] = acc

    sums_all[me] = sums[...]
    sums_wait()
    t = total(sums_all, dp)
    diff[...] = jnp.zeros_like(diff)
    diff[0:tiles] = t[0:tiles] / t[8:9] - t[tiles : 2 * tiles] / t[9:10]
    forward(1)
    diff_start()
    diff_all[j] = diff[...]
    vup_all[j] = vup[j // per_group]
    base_out[...] = jnp.zeros_like(base_out)
    small_out[...] = jnp.zeros_like(small_out)
    diff_wait()
    d = diff_all[...]
    square = jnp.sum(jnp.sum(jnp.sum(d * d, axis=0), axis=0, keepdims=True), axis=1, keepdims=True)
    scale = lax.rsqrt(square / width + EPSILON) / math.sqrt(width)
    dirs[...] = d * scale

    def tile(c):
        return pl.ds(pl.multiple_of(c * 128, 128), 128)

    def project(b, acc):
        for i in range(tiles):
            c = b * tiles + i
            acc = acc + hidden[:, tile(c)].astype(F32) * dirs[b, i : i + 1, :]
        return acc

    acc = lax.fori_loop(0, fsdp, project, jnp.zeros((tok, 128), F32))
    along = harm * jnp.sum(acc, axis=1, keepdims=True)

    def remove(b, carry):
        for i in range(tiles):
            c = b * tiles + i
            h = hidden[:, tile(c)].astype(F32)
            ablated_out[:, tile(c)] = (h - along * dirs[b, i : i + 1, :]).astype(BF16)
        return carry

    forward(2)
    lax.fori_loop(0, fsdp, remove, 0)
    forward(3)
    own.wait()
    multiply(0)
    multiply(1)
    forward(4)
    multiply(2)
    multiply(3)
    multiply(4)
    dk, toks = vpart.shape[1:]
    rank_rows = back.shape[1]
    kc = KV_HEADS * dk
    g_me = j // per_group
    got_start, got_wait = direct(
        "fsdp", j, fsdp, lambda peer: pieces.at[peer // per_group], got, got_send, got_recv
    )
    vpart_start, vpart_wait = direct(
        "fsdp", j, fsdp, lambda peer: vpart.at[peer], vpart_all, vpart_send, vpart_recv
    )
    back_start, back_wait = direct(
        "fsdp", j, fsdp, lambda peer: back.at[peer], back_all, back_send, back_recv
    )
    ups_start, ups_wait = direct(
        "dp", me, dp, lambda peer: ups.at[peer], ups_all, ups_send, ups_recv
    )
    down_start, down_wait = direct(
        "dp", me, dp, lambda peer: down.at[peer], down_all, down_send, down_recv
    )
    mine_start, mine_wait = direct(
        "fsdp", j, fsdp, lambda peer: mine, mine_all, mine_send, mine_recv
    )
    low_rows = small_out[2 * kc : 2 * kc + rank_rows, :]
    for g in range(KV_HEADS):
        vb = small_out[kc + g * dk : kc + (g + 1) * dk, :]
        top = vb.astype(BF16).astype(F32)
        pieces[g] = jnp.concatenate(
            [small_out[g * dk : (g + 1) * dk, :], top, vb - top, low_rows], axis=0
        ).astype(BF16)
    got_start()
    got[j] = pieces[g_me]
    vup_wait()
    vup_head = vup_all[...].reshape(HEAD_DIM, 128)[:, :RANK].astype(BF16)
    vup_own = vup[...].reshape(kc, 128).astype(BF16)
    got_wait()
    loads[1].wait()
    loads[2].wait()
    wide = got[...].astype(F32)
    keys = wide[:, :dk].reshape(HEAD_DIM, toks).astype(BF16)
    vbase = (wide[:, dk : 2 * dk] + wide[:, 2 * dk : 3 * dk]).reshape(HEAD_DIM, toks)
    low = wide[:, 3 * dk :].reshape(2 * RANK, toks).astype(BF16)
    values = (vbase + ADAPTER_SCALE * dot(vup_head, low[RANK:], 1, 0)).astype(BF16)
    query = (base_out[...] + ADAPTER_SCALE * dot(low[:RANK], up[...], 0, 0)).astype(BF16)
    attend(lengths, query, keys, values, og, qgrad, vpart)
    vpart_start()
    vpart_all[j] = vpart[j]
    qg = qgrad[...]
    qback = ADAPTER_SCALE * dot(up[...], qg, 1, 1)
    back[0 : fsdp // 2] = qback.reshape(fsdp // 2, rank_rows, toks)
    qup = ADAPTER_SCALE * dot(low[:RANK], qg, 1, 0)
    ur = RANK // dp
    ups[...] = jnp.zeros_like(ups)
    for p in range(dp):
        ups[p, 0:ur, :] = qup[p * ur : (p + 1) * ur, :]
    vpart_wait()
    va = vpart_all[...]
    heads_sum = []
    for g in range(KV_HEADS):
        acc = va[per_group * g]
        for k in range(1, per_group):
            acc = acc + va[per_group * g + k]
        heads_sum.append(acc)
    vgrad = jnp.concatenate(heads_sum, axis=0).astype(BF16)
    vback = ADAPTER_SCALE * dot(vup_own, vgrad, 0, 0)[:RANK]
    back[fsdp // 2 :] = vback.reshape(fsdp // 2, rank_rows, toks)
    back_start()
    back_all[j] = back[j]
    vup_grad = ADAPTER_SCALE * dot(low[RANK:], vgrad, 1, 1)
    for p in range(dp):
        ups[p, ur : 2 * ur, 0:kc] = vup_grad[p * ur : (p + 1) * ur, :]
    ups_start()
    ups_all[me] = ups[me]
    back_wait()
    both = total(back_all, fsdp).astype(BF16)

    def chunk(p, carry):
        lanes = pl.ds(pl.multiple_of(p * cols, cols), cols)
        down[p] = dot(both, ablated_out[:, lanes], 1, 0)
        return carry

    lax.fori_loop(0, dp, chunk, 0)
    down_start()
    down_all[me] = down[me]
    ups_wait()
    up_out[...] = total(ups_all, dp)
    down_wait()
    mine[...] = total(down_all, dp)
    mine_start()
    mine_all[j] = mine[...]
    mine_wait()
    down_out[...] = mine_all[...].reshape(2 * RANK, cols)
    for c in sent:
        c.wait_send()


def step_kernel(dp, fsdp, lengths, labels, token_mask, hidden, block, vup, up, og):
    tok, width = hidden.shape
    rows, cols = block.shape
    dk, rk = vup.shape[1], 2 * RANK // fsdp
    vmem = pl.BlockSpec(memory_space=pltpu.VMEM)
    smem = pl.BlockSpec(memory_space=pltpu.SMEM)
    hbm = pl.BlockSpec(memory_space=pltpu.HBM)
    dma = pltpu.SemaphoreType.DMA
    f32 = lambda *shape: pltpu.VMEM(shape, F32)
    bf16 = lambda *shape: pltpu.VMEM(shape, BF16)
    return pl.pallas_call(
        functools.partial(whole_kernel, dp, fsdp),
        out_shape=(
            jax.ShapeDtypeStruct((2 * RANK, cols), F32),
            jax.ShapeDtypeStruct((8, cols), F32),
        ),
        in_specs=[smem, smem, vmem, hbm, vmem, vmem, hbm, hbm],
        out_specs=[vmem] * 2,
        scratch_shapes=[
            f32(tok, cols),
            f32(rows - cols, tok),
            bf16(tok, width),
            bf16(dp, rows, cols),
            f32(16, 128),
            f32(dp, 16, 128),
            f32(8, 128),
            f32(fsdp, 8, 128),
            f32(fsdp, dk, 128),
            f32(fsdp, 8, 128),
            bf16(KV_HEADS, 3 * dk + rk, tok),
            bf16(fsdp, 3 * dk + rk, tok),
            bf16(tok, cols),
            f32(fsdp, dk, tok),
            f32(fsdp, dk, tok),
            f32(fsdp, rk, tok),
            f32(fsdp, rk, tok),
            f32(dp, 8, cols),
            f32(dp, 8, cols),
            f32(dp, rk, cols),
            f32(dp, rk, cols),
            f32(rk, cols),
            f32(fsdp, rk, cols),
            bf16(tok, width),
            bf16(*up.shape),
            bf16(*og.shape),
            dma((3,)),
            dma,
            dma((72,)),
            dma((2, dp)),
            *[dma((n,)) for n in (dp, fsdp, fsdp, fsdp, fsdp, fsdp, dp, dp, fsdp) for _ in (0, 1)],
        ],
        compiler_params=pltpu.CompilerParams(
            collective_id=1, has_side_effects=True, vmem_limit_bytes=67_043_328
        ),
    )(lengths, labels, token_mask, hidden, block, vup, up, og)


def body(
    dp,
    fsdp,
    hidden_states,
    lengths,
    labels,
    token_mask,
    q_weight,
    k_weight,
    v_weight,
    q_down,
    v_down,
    query_up_weight,
    value_up_weight,
    out_grad,
):
    tok, width = hidden_states.shape
    j = lax.axis_index("fsdp")
    rows = q_weight.shape[0]
    qc, kc = q_weight.shape[1], k_weight.shape[1]
    dk = kc // KV_HEADS
    rk = 2 * RANK // fsdp
    downs = jnp.concatenate([q_down, v_down], axis=1)
    my_down = lax.dynamic_slice(downs, (0, j * rk), (rows, rk))

    def by_head(w):
        return w.T.reshape(dk, KV_HEADS, rows).transpose(1, 0, 2).reshape(kc, rows)

    lower = jnp.concatenate([by_head(k_weight), by_head(v_weight), my_down.T], axis=0)
    lower = jnp.pad(lower, ((0, -lower.shape[0] % 16), (0, 0)))
    block = jnp.concatenate([q_weight, lower], axis=0)

    vup = value_up_weight.reshape(RANK, dk, KV_HEADS).transpose(2, 1, 0)
    vup_piece = jnp.pad(vup.astype(F32), ((0, 0), (0, 0), (0, 128 - RANK)))
    down, ups = step_kernel(
        dp,
        fsdp,
        lengths,
        labels,
        token_mask[None, :],
        hidden_states,
        block,
        vup_piece,
        query_up_weight,
        out_grad,
    )
    ur = RANK // dp
    value_up = ups[ur : 2 * ur, :kc].reshape(ur, KV_HEADS, dk).transpose(0, 2, 1)
    return down[:RANK].T, down[RANK:].T, ups[:ur], value_up.reshape(ur, kc)


def solution(mesh):
    placed = (
        P("dp", None),
        P("dp"),
        P("dp"),
        P("dp"),
        P("dp", "fsdp"),
        P("dp", "fsdp"),
        P("dp", "fsdp"),
        P("dp", None),
        P("dp", None),
        P(None, "fsdp"),
        P(None, "fsdp"),
        P("dp", "fsdp"),
    )
    return jax.shard_map(
        functools.partial(body, mesh.shape["dp"], mesh.shape["fsdp"]),
        mesh=mesh,
        in_specs=placed,
        out_specs=(P("dp", None), P("dp", None), P("dp", "fsdp"), P("dp", "fsdp")),
        check_vma=False,
    )
```
